256 devices in a mesh: dp: 64 (over z, y, x_hi), seq: 4 (over x_lo, core).
Axes of the slice: x: 4 (x_hi: 2, x_lo: 2; x = x_hi * 2 + x_lo), y: 4, z: 8, core: 2. Of those that a mesh axis runs over, the one named last changes fastest.
Arguments:
- queries: bfloat16 [32768, 2560], P(('dp', 'seq')), may hold values from -400 to 400
- key_states: bfloat16 [32768, 2560], P(('dp', 'seq')), may hold values from -400 to 400
- value_states: bfloat16 [32768, 2560], P(('dp', 'seq')), may hold values from -6 to 6
- query_tangent: bfloat16 [32768, 2560], P(('dp', 'seq')), may hold values from -6 to 6
- key_tangent: bfloat16 [32768, 2560], P(('dp', 'seq')), may hold values from -6 to 6
- value_tangent: bfloat16 [32768, 2560], P(('dp', 'seq')), may hold values from -6 to 6
- query_gain: float32 [2560], replicated, may hold values from 0.25 to 1.75
- key_gain: float32 [2560], replicated, may hold values from 0.25 to 1.75
- out_weight: bfloat16 [2560, 5120], P('seq', 'dp'), may hold values from -0.125 to 0.125
Outputs:
- projected: bfloat16 [32768, 5120], P(('dp', 'seq'))
- projected_tangent: bfloat16 [32768, 5120], P(('dp', 'seq'))
The draws below stay inside these ranges and needn't reach their ends.
All inputs are finite; a program needn't handle non-finite values.
Results may differ from the reference program's by a relative error of at most 0.012.
The reference program's roundings to bfloat16 on the way count: a program that leaves them out, or rounds other values in their place, can miss the bound.
Values may be sent and summed in bfloat16 or wider, within the bound.
A program may use at most 128 MiB of HBM per device.

```python
import math
import jax
import jax.numpy as jnp
from jax import lax

D = 5120
HEADS = 20
HDIM = 128
LEN = 512
CLIPS = 64
TOKENS = 32768
HW = 2560


def scaled_field(key):
    first, second, third = jax.random.split(key, 3)
    values = jnp.clip(jax.random.normal(first, (TOKENS, HW), jnp.float32), -4.0, 4.0)
    row_scale = jnp.exp(jax.random.uniform(second, (TOKENS, 1), jnp.float32) * math.log(10.0))
    column_scale = jnp.exp(jax.random.uniform(third, (1, HW), jnp.float32) * math.log(10.0))
    return values * row_scale * column_scale


def draw_queries(key, part):
    values = scaled_field(jax.random.fold_in(key, 1))
    return values.astype(jnp.bfloat16)


def draw_key_states(key, part):
    values = scaled_field(jax.random.fold_in(key, 2))
    return values.astype(jnp.bfloat16)


def levels(rng, shape, cuts, least, top_value):
    loudness, own = 1.0, jax.random.fold_in(rng, 6)
    for axis_at, blocks in cuts:
        heights = jnp.exp(jax.random.uniform(jax.random.fold_in(own, axis_at), (blocks,), jnp.float32, least / len(cuts), top_value / len(cuts)))
        loudness = loudness * jnp.repeat(heights, shape[axis_at] // blocks).reshape([-1 if axis == axis_at else 1 for axis in range(len(shape))])
    return loudness


def noise(stream_key, shape, deviation, limit, cuts=(), held_as=jnp.bfloat16):
    loudness = levels(stream_key, shape, cuts, -0.22, 0.18) if cuts else 1.0
    entries = jax.random.normal(stream_key, shape, jnp.float32) * deviation * loudness
    return jnp.minimum(jnp.maximum(entries, -limit), limit).astype(held_as)


def setup_inputs(seed: int = 0) -> dict:
    streams_of = jax.random.split(jax.random.key(seed), 10)
    return {
        "queries": draw_queries(jax.random.fold_in(streams_of[9], 71), 0),
        "key_states": draw_key_states(jax.random.fold_in(streams_of[9], 71), 0),
        "value_states": noise(streams_of[2], (TOKENS, HW), 1.0, 6.0, ((0, 256),)),
        "query_tangent": noise(streams_of[3], (TOKENS, HW), 1.0, 6.0, ((0, 256),)),
        "key_tangent": noise(streams_of[4], (TOKENS, HW), 1.0, 6.0, ((0, 256),)),
        "value_tangent": noise(streams_of[5], (TOKENS, HW), 1.0, 6.0, ((0, 256),)),
        "query_gain": jnp.clip(1.0 + 0.15 * jax.random.normal(streams_of[6], (HW,), jnp.float32), 0.25, 1.75),
        "key_gain": jnp.clip(1.0 + 0.15 * jax.random.normal(streams_of[7], (HW,), jnp.float32), 0.25, 1.75),
        "out_weight": noise(streams_of[8], (HW, D), HW ** -0.5, 0.125, ((0, 4), (1, 64))),
    }


def rms_tangent(primal, tangent, gain):
    primal_f = primal.astype(jnp.float32)
    tangent_f = tangent.astype(jnp.float32)
    inverse = lax.rsqrt(lax.optimization_barrier(jnp.mean(primal_f * primal_f, axis=-1, keepdims=True)) + 1e-06)
    across = lax.optimization_barrier(jnp.mean(primal_f * tangent_f, axis=-1, keepdims=True))
    normed = (primal_f * inverse * gain).astype(jnp.bfloat16)
    normed_tangent = (gain * (tangent_f * inverse - primal_f * inverse ** 3 * across)).astype(jnp.bfloat16)
    return (normed, normed_tangent)

def widen(array):
    return array.astype(jnp.float32)

def attend(query_normed, query_dual, key_normed, key_dual, value_plain, value_dual):
    factor = HDIM ** (-0.5)
    scores = jnp.einsum('qhd,khd->hqk', widen(query_normed), widen(key_normed)) * factor
    dual_scores = (jnp.einsum('qhd,khd->hqk', widen(query_dual), widen(key_normed)) + jnp.einsum('qhd,khd->hqk', widen(query_normed), widen(key_dual))) * factor
    peak = lax.optimization_barrier(jnp.max(scores, axis=-1, keepdims=True))
    raised = jnp.exp(scores - peak)
    probs = raised / lax.optimization_barrier(jnp.sum(raised, axis=-1, keepdims=True))
    spread = probs * (dual_scores - lax.optimization_barrier(jnp.sum(probs * dual_scores, axis=-1, keepdims=True)))
    probs_low, spread_low = lax.optimization_barrier((probs.astype(jnp.bfloat16), spread.astype(jnp.bfloat16)))
    attn = jnp.einsum('hqk,khd->qhd', widen(probs_low), widen(value_plain)).astype(jnp.bfloat16)
    dual_attn = (jnp.einsum('hqk,khd->qhd', widen(probs_low), widen(value_dual)) + jnp.einsum('hqk,khd->qhd', widen(spread_low), widen(value_plain))).astype(jnp.bfloat16)
    return (attn, dual_attn)

def reference(queries, key_states, value_states, query_tangent, key_tangent, value_tangent, query_gain, key_gain, out_weight):
    query_normed, query_dual = rms_tangent(queries, query_tangent, query_gain)
    key_normed, key_dual = rms_tangent(key_states, key_tangent, key_gain)
    query_normed, query_dual, key_normed, key_dual = lax.optimization_barrier((query_normed, query_dual, key_normed, key_dual))

    def per_clip(pieces):
        shaped = [array.reshape(LEN, HEADS, HDIM) for array in pieces]
        attn, dual_attn = attend(shaped[0], shaped[1], shaped[2], shaped[3], shaped[4], shaped[5])
        plain_out = jnp.dot(attn.reshape(LEN, HEADS * HDIM), out_weight, preferred_element_type=jnp.float32).astype(jnp.bfloat16)
        dual_out = jnp.dot(dual_attn.reshape(LEN, HEADS * HDIM), out_weight, preferred_element_type=jnp.float32).astype(jnp.bfloat16)
        return (plain_out, dual_out)
    clips = tuple((array.reshape(CLIPS, LEN, HEADS * HDIM) for array in (query_normed, query_dual, key_normed, key_dual, value_states, value_tangent)))
    plain_all, dual_all = lax.map(per_clip, clips)
    return (plain_all.reshape(TOKENS, D), dual_all.reshape(TOKENS, D))
```

```python
import jax
import jax.numpy as jnp
from jax import lax
from jax.experimental import pallas as pl
from jax.experimental.pallas import tpu as pltpu
from jax.sharding import PartitionSpec as P

HDIM = 128
NZ, NY = 8, 4
ROWS = 128
BLK = 640
UNIT = 80
PLANE = 640
EPS = 1e-06
MESH = pl.DeviceIdType.MESH
BF16 = jnp.bfloat16
F32 = jnp.float32


def rms_tangent(primal_ref, tangent_ref, gain_ref, normed_ref, dual_ref):
    width = primal_ref.shape[1]
    for row in range(0, ROWS, 32):
        rows = pl.ds(row, 32)
        primal = primal_ref[rows, :].astype(F32)
        tangent = tangent_ref[rows, :].astype(F32)
        inverse = lax.rsqrt(jnp.sum(primal * primal, axis=-1, keepdims=True) * (1.0 / width) + EPS)
        across = jnp.sum(primal * tangent, axis=-1, keepdims=True) * (1.0 / width)
        pull = inverse * inverse * inverse * across
        gain = gain_ref[...]
        normed = (primal * inverse * gain).astype(BF16)
        dual = (gain * (tangent * inverse - primal * pull)).astype(BF16)
        for block in range(4):
            normed_ref[block, rows, :] = normed[:, block * BLK : (block + 1) * BLK]
            dual_ref[block, rows, :] = dual[:, block * BLK : (block + 1) * BLK]


def kernel(
    q_in,
    dq_in,
    k_in,
    dk_in,
    v_in,
    dv_in,
    q_gain,
    k_gain,
    w_in,
    out,
    dual_out,
    w_all,
    qn,
    dqn,
    kn,
    dkn,
    q_all,
    dq_all,
    k_all,
    dk_all,
    v_all,
    dv_all,
    attn,
    acc,
    give,
    got,
    done,
    w_recv,
    w_send,
    first_sem,
    kv_recv,
    kv_send,
    q_recv,
    q_send,
    own_sem,
    part_recv,
    part_send,
    out_sem,
):
    dp = lax.axis_index("dp")
    seq = lax.axis_index("seq")
    z, y, hi = dp // 8, lax.rem(dp // 2, 4), lax.rem(dp, 2)
    lo, core = seq // 2, lax.rem(seq, 2)
    way = 1 - 2 * core

    def unit(zz, yy, hh):
        return zz * 8 + yy * 2 + hh

    def z_at(off):
        return lax.rem(z + off * way + NZ, NZ)

    def y_at(off):
        return lax.rem(y + off * way + NY, NY)

    side = {
        "zf": (unit(z_at(1), y, hi), seq),
        "zb": (unit(z_at(-1), y, hi), seq),
        "yf": (unit(z, y_at(1), hi), seq),
        "yb": (unit(z, y_at(-1), hi), seq),
        "hi": (unit(z, y, 1 - hi), (1 - lo) * 2 + core),
        "lo": (dp, (1 - lo) * 2 + core),
        "cross": (dp, (1 - lo) * 2 + 1 - core),
        "mate": (dp, lo * 2 + 1 - core),
    }

    barrier = pltpu.get_barrier_semaphore()
    for target in side.values():
        pl.semaphore_signal(barrier, inc=1, device_id=target, device_id_type=MESH)
    pl.semaphore_wait(barrier, len(side))

    def remote(src, dst, send_sem, recv_sem, to):
        return pltpu.make_async_remote_copy(
            src_ref=src,
            dst_ref=dst,
            send_sem=send_sem,
            recv_sem=recv_sem,
            device_id=side[to],
            device_id_type=MESH,
        )

    own_w = pltpu.make_async_copy(w_in, w_all.at[lo, dp], first_sem.at[0])
    own_w.start()
    lo_w = remote(w_in, w_all.at[lo, dp], first_sem.at[1], first_sem.at[2], "lo")
    lo_w.start()

    def mine(group):
        return core + 2 * group

    def theirs(group):
        return 1 - core + 2 * group

    def columns(block):
        return pl.ds(pl.multiple_of(block * BLK, 128), BLK)

    def kv_source(tensor, block):
        if tensor == 0:
            return kn.at[block]
        if tensor == 1:
            return dkn.at[block]
        return (v_in if tensor == 2 else dv_in).at[:, columns(block)]

    kv_home = (k_all, dk_all, v_all, dv_all)
    kv_to = ("mate", "lo", "cross")

    def kv_copy(group, tensor, which):
        to = kv_to[which]
        block = mine(group) if to == "lo" else theirs(group)
        return remote(
            kv_source(tensor, block),
            kv_home[tensor].at[group, pl.ds((which + 1) * ROWS, ROWS), :],
            kv_send.at[group, tensor, which],
            kv_recv.at[group, tensor, which],
            to,
        )

    def kv_own(group, tensor):
        return pltpu.make_async_copy(
            kv_source(tensor, mine(group)),
            kv_home[tensor].at[group, pl.ds(0, ROWS), :],
            own_sem.at[group, tensor],
        )

    q_from, q_home = (qn, dqn), (q_all, dq_all)

    def q_copy(group, tensor):
        return remote(
            q_from[tensor].at[theirs(group)],
            q_home[tensor].at[group, pl.ds(ROWS, ROWS), :],
            q_send.at[group, tensor],
            q_recv.at[group, tensor],
            "mate",
        )

    def q_own(group, tensor):
        return pltpu.make_async_copy(
            q_from[tensor].at[mine(group)],
            q_home[tensor].at[group, pl.ds(0, ROWS), :],
            own_sem.at[group, 4 + tensor],
        )

    def start_kv(group, tensors):
        for which in (1, 2, 0):
            for tensor in tensors:
                kv_copy(group, tensor, which).start()
        for tensor in tensors:
            kv_own(group, tensor).start()

    def start_q(group):
        for tensor in range(2):
            q_copy(group, tensor).start()
            q_own(group, tensor).start()

    def wait_group(group):
        for tensor in range(4):
            kv_own(group, tensor).wait()
            for which in range(3):
                kv_copy(group, tensor, which).wait_recv()
        for tensor in range(2):
            q_own(group, tensor).wait()
            q_copy(group, tensor).wait_recv()

    start_kv(0, (2, 3))
    rms_tangent(k_in, dk_in, k_gain, kn, dkn)

    def piece(stream, source):
        if stream == 0:
            return w_all.at[:, source, pl.ds(0, 32), :]
        return w_all.at[stream - 1, source, pl.ds(32, 48), :]

    def w_copy(stream, source, to):
        where = piece(stream, source)
        return remote(where, where, w_send.at[stream], w_recv.at[stream, source], to)

    def pass_on(stream, source, targets):
        for to in targets:
            w_copy(stream, source, to).start()

    def arrive(stream, source, targets=()):
        w_copy(stream, source, "zf").wait_recv()
        pass_on(stream, source, targets)

    y_offs = (0, 1, -1, 2)

    def src(zo, yo, flip):
        return unit(z_at(-zo), y_at(-yo), 1 - hi if flip else hi)

    def z_next(zo):
        if zo > 0:
            return ("zf",) if zo < 4 else ()
        return ("zb",) if zo > -3 else ()

    events = []

    def note(*what):
        events.append(lambda: arrive(*what))

    def ring(r):
        return (0,) if r == 0 else ((4,) if r == 4 else (r, -r))

    def s0_z(r):
        for zo in ring(r):
            note(0, src(zo, 0, False), z_next(zo) + ("yf", "yb", "hi"))

    def s0_y(r):
        for zo in ring(r):
            note(0, src(zo, 1, False), ("yf", "hi"))
            note(0, src(zo, -1, False), ("hi",))
        for zo in ring(r):
            note(0, src(zo, 2, False), ("hi",))

    def s0_end(r):
        for zo in ring(r):
            for yo in y_offs:
                note(0, src(zo, yo, True), ())

    def s1_y():
        for flip in (False, True):
            note(1, src(0, 1, flip), ("yf", "zf", "zb"))
            note(1, src(0, -1, flip), ("zf", "zb"))
        for flip in (False, True):
            note(1, src(0, 2, flip), ("zf", "zb"))

    def s1_z(r):
        for yo in y_offs:
            for flip in (False, True):
                for zo in ring(r):
                    note(1, src(zo, yo, flip), z_next(zo))

    def s2_z(r):
        for flip in (False, True):
            for zo in ring(r):
                note(2, src(zo, 0, flip), z_next(zo) + ("yf", "yb"))

    def s2_y(r):
        for zo in ring(r):
            for flip in (False, True):
                note(2, src(zo, 1, flip), ("yf",))
                note(2, src(zo, -1, flip), ())
        for zo in ring(r):
            for flip in (False, True):
                note(2, src(zo, 2, flip), ())

    own_w.wait()
    lo_w.wait_recv()
    pass_on(1, dp, ("hi",))
    pass_on(2, dp, ("hi",))
    pass_on(0, dp, ("zf", "zb", "yf", "yb", "hi"))
    pass_on(1, dp, ("yf", "yb", "zf", "zb"))
    pass_on(2, dp, ("zf", "zb", "yf", "yb"))

    rms_tangent(q_in, dq_in, q_gain, qn, dqn)
    start_kv(0, (0, 1))
    start_q(0)
    start_q(1)
    start_kv(1, (2, 3))
    start_kv(1, (0, 1))

    factor = HDIM ** (-0.5)
    nt = (((1,), (1,)), ((), ()))

    def head(group, index):
        cols = pl.ds(index * HDIM, HDIM)
        queries, dual_queries = q_all[group, :, cols], dq_all[group, :, cols]
        keys, dual_keys = k_all[group, :, cols], dk_all[group, :, cols]
        values, dual_values = v_all[group, :, cols], dv_all[group, :, cols]
        scores = lax.dot_general(queries, keys, nt, preferred_element_type=F32) * factor
        dual_scores = (
            lax.dot_general(
                jnp.concatenate([dual_queries, queries], axis=1),
                jnp.concatenate([keys, dual_keys], axis=1),
                nt,
                preferred_element_type=F32,
            )
            * factor
        )
        raised = jnp.exp(scores - jnp.max(scores, axis=-1, keepdims=True))
        probs = raised * (1.0 / jnp.sum(raised, axis=-1, keepdims=True))
        spread = probs * (dual_scores - jnp.sum(probs * dual_scores, axis=-1, keepdims=True))
        low = probs.astype(BF16)
        both = jnp.dot(
            low, jnp.concatenate([values, dual_values], axis=1), preferred_element_type=F32
        )
        dual = both[:, HDIM:] + jnp.dot(spread.astype(BF16), values, preferred_element_type=F32)
        plain = both[:, :HDIM].astype(BF16)
        dual = dual.astype(BF16)
        for owner in range(2):
            rows = slice(owner * ROWS, (owner + 1) * ROWS)
            attn[group, pl.ds(owner * 256, ROWS), cols] = plain[rows]
            attn[group, pl.ds(owner * 256 + ROWS, ROWS), cols] = dual[rows]

    plane_offs = (0, -1, 1, -2, 2, -3, 3, 4)

    def plane_of(index):
        return lax.rem(z + plane_offs[index] + NZ, NZ)

    def product(group, plane):
        first = pl.multiple_of(plane * 8, 8)
        weight = w_all[group, pl.ds(first, 8)].reshape(PLANE, BLK)
        return lax.dot_general(attn[group], weight, nt, preferred_element_type=F32)

    def half_one(index):
        acc[index] = product(0, plane_of(index))

    def part_copy(plane, index):
        return remote(
            give.at[index], got.at[plane], part_send.at[index], part_recv.at[plane], "mate"
        )

    def half_two(index):
        plane = plane_of(index)
        total = acc[index] + product(1, plane)
        acc[index, pl.ds(0, 256), :] = total[:256]
        give[index] = total[256:].astype(BF16)
        part_copy(plane, index).start()

    def out_copies(index):
        plane = plane_of(index)
        cols = pl.ds(pl.multiple_of(plane * PLANE, 128), PLANE)
        return [
            pltpu.make_async_copy(
                done.at[index, pl.ds(half * ROWS, ROWS), :],
                (out, dual_out)[half].at[:, cols],
                out_sem.at[index, half],
            )
            for half in range(2)
        ]

    def finish(index):
        plane = plane_of(index)
        part_copy(plane, index).wait_recv()
        done[index] = (acc[index, pl.ds(0, 256), :] + got[plane].astype(F32)).astype(BF16)
        for copy in out_copies(index):
            copy.start()

    def weave(tasks):
        pending, count = list(events), len(tasks)
        events.clear()
        at = 0
        for place, event in enumerate(pending):
            event()
            while at < count and (at + 1) * len(pending) <= (place + 1) * count:
                tasks[at]()
                at += 1
        for task in tasks[at:]:
            task()

    note(1, src(0, 0, True), ("yf", "yb", "zf", "zb"))
    note(2, src(0, 0, True), ("zf", "zb", "yf", "yb"))
    s0_z(1)
    s1_y()
    s0_y(0)
    s2_z(1)
    s2_y(0)
    s0_z(2)
    s0_y(1)
    s1_z(1)
    s0_end(0)
    s2_z(2)
    s2_y(1)
    s0_z(3)
    s0_y(2)
    s1_z(2)
    s0_end(1)
    s2_z(3)
    s2_y(2)
    weave([])
    wait_group(0)
    s0_z(4)
    s0_y(3)
    s1_z(3)
    s0_end(2)
    s2_z(4)
    s2_y(3)
    weave([lambda i=i: head(0, i) for i in range(5)])
    s0_y(4)
    s1_z(4)
    s0_end(3)
    s2_y(4)
    s0_end(4)
    weave([lambda i=i: half_one(i) for i in range(5)])
    wait_group(1)
    for i in range(5):
        head(1, i)
    for i in range(5, 8):
        half_one(i)
    for i in range(8):
        half_two(i)
        if i > 0:
            finish(i - 1)
    finish(7)

    lo_w.wait_send()
    for group in range(2):
        for tensor in range(4):
            for which in range(3):
                kv_copy(group, tensor, which).wait_send()
        for tensor in range(2):
            q_copy(group, tensor).wait_send()
    sent = (w_all.at[:, pl.ds(0, 63), pl.ds(0, 32), :],) + tuple(
        w_all.at[j, pl.ds(0, 63), pl.ds(32, 48), :] for j in range(2)
    )
    for stream in range(3):
        pltpu.make_async_copy(sent[stream], sent[stream], w_send.at[stream]).wait()
    for index in range(8):
        part_copy(plane_of(index), index).wait_send()
        for copy in out_copies(index):
            copy.wait()


def body(q, k, v, dq, dk, dv, q_gain, k_gain, weight):
    rows, width = q.shape
    vmem = pl.BlockSpec(memory_space=pltpu.VMEM)
    hbm = pl.BlockSpec(memory_space=pl.ANY)
    sem = pltpu.SemaphoreType.DMA
    kv = pltpu.VMEM((2, 4 * ROWS, BLK), BF16)
    qs = pltpu.VMEM((2, 2 * ROWS, BLK), BF16)
    normed = pltpu.VMEM((4, ROWS, BLK), BF16)
    shape = jax.ShapeDtypeStruct((rows, 2 * width), BF16)
    return pl.pallas_call(
        kernel,
        out_shape=(shape, shape),
        in_specs=[vmem] * 4 + [hbm] * 2 + [vmem] * 2 + [hbm],
        out_specs=(hbm, hbm),
        scratch_shapes=[
            pltpu.VMEM((2, 64, UNIT, BLK), BF16),
            normed,
            normed,
            normed,
            normed,
            qs,
            qs,
            kv,
            kv,
            kv,
            kv,
            pltpu.VMEM((2, 4 * ROWS, BLK), BF16),
            pltpu.VMEM((8, 4 * ROWS, PLANE), F32),
            pltpu.VMEM((8, 2 * ROWS, PLANE), BF16),
            pltpu.VMEM((8, 2 * ROWS, PLANE), BF16),
            pltpu.VMEM((8, 2 * ROWS, PLANE), BF16),
            sem((3, 64)),
            sem((3,)),
            sem((3,)),
            sem((2, 4, 3)),
            sem((2, 4, 3)),
            sem((2, 2)),
            sem((2, 2)),
            sem((2, 6)),
            sem((8,)),
            sem((8,)),
            sem((8, 2)),
        ],
        compiler_params=pltpu.CompilerParams(
            collective_id=0, has_side_effects=True, vmem_limit_bytes=60 * 1024 * 1024
        ),
        name="tangent_attention",
    )(q, dq, k, dk, v, dv, q_gain.reshape(1, width), k_gain.reshape(1, width), weight.T)


def solution(mesh):
    tokens = P(("dp", "seq"), None)
    return jax.shard_map(
        body,
        mesh=mesh,
        in_specs=(tokens,) * 6 + (P(), P(), P("seq", "dp")),
        out_specs=(tokens, tokens),
        check_vma=False,
    )
```

```python
import jax
import jax.numpy as jnp
from jax import lax
from jax.experimental import pallas as pl
from jax.experimental.pallas import tpu as pltpu
from jax.sharding import PartitionSpec as P

HDIM = 128
NZ, NY = 8, 4
ROWS = 128
BLK = 640
UNIT = 80
PLANE = 640
EPS = 1e-06
MESH = pl.DeviceIdType.MESH
BF16 = jnp.bfloat16
F32 = jnp.float32

Z_OFFS = (0, 1, -1, 2, -2, 3, -3, 4)
Y_OFFS = (0, 1, -1, 2)
SECOND, KEY_NORM, KEYS, QUERY_NORM, QUERIES, HEAD = 200, 201, 202, 203, 204, 300
FIRST, MIDDLE, LAST, REST, WHOLE, FINISH = 400, 410, 420, 430, 440, 450
ORDER = (
    201, 202, 72, 80, 66, 68, 65, 200, 203, 204, 88, 70, 96, 69, 1, 4, 74, 67, 82, 129, 2, 132, 76,
    84, 130, 73, 81, 71, 300, 5, 8, 16, 133, 131, 6, 136, 144, 3, 134, 104, 86, 78, 112, 10, 12, 9,
    301, 77, 85, 18, 20, 17, 90, 83, 135, 140, 7, 75, 98, 138, 148, 137, 145, 146, 11, 14, 92, 302,
    100, 22, 13, 89, 97, 141, 142, 19, 79, 87, 149, 139, 147, 21, 24, 32, 150, 303, 152, 143, 160,
    15, 151, 120, 102, 23, 28, 26, 94, 101, 25, 93, 36, 99, 34, 106, 156, 114, 304, 33, 154, 91,
    164, 161, 162, 400, 29, 30, 153, 116, 401, 38, 27, 108, 113, 402, 158, 165, 105, 103, 37, 305,
    163, 157, 95, 166, 48, 35, 155, 40, 176, 31, 168, 118, 167, 39, 110, 404, 117, 52, 50, 306, 109,
    115, 49, 44, 159, 122, 177, 403, 180, 41, 107, 119, 42, 172, 169, 53, 178, 124, 181, 121, 307,
    170, 111, 51, 56, 410, 173, 54, 184, 179, 411, 45, 126, 46, 412, 125, 413, 123, 171, 43, 185,
    414, 60, 127, 182, 308, 57, 188, 174, 55, 189, 58, 186, 183, 406, 47, 175, 405, 187, 61, 309,
    62, 190, 420, 59, 421, 191, 422, 423, 450, 424, 451, 452, 63, 435, 453, 454, 436, 447, 455, 456,
    457,
)


def rms_tangent(primal_ref, tangent_ref, gain_ref, normed_ref, dual_ref):
    width = primal_ref.shape[1]
    for row in range(0, ROWS, 32):
        rows = pl.ds(row, 32)
        primal = primal_ref[rows, :].astype(F32)
        tangent = tangent_ref[rows, :].astype(F32)
        inverse = lax.rsqrt(jnp.sum(primal * primal, axis=-1, keepdims=True) * (1.0 / width) + EPS)
        across = jnp.sum(primal * tangent, axis=-1, keepdims=True) * (1.0 / width)
        pull = inverse * inverse * inverse * across
        gain = gain_ref[...].reshape(1, width)
        normed = (primal * inverse * gain).astype(BF16)
        dual = (gain * (tangent * inverse - primal * pull)).astype(BF16)
        for block in range(4):
            normed_ref[block, rows, :] = normed[:, block * BLK : (block + 1) * BLK]
            dual_ref[block, rows, :] = dual[:, block * BLK : (block + 1) * BLK]


def kernel(
    q_in,
    dq_in,
    k_in,
    dk_in,
    v_in,
    dv_in,
    q_gain,
    k_gain,
    w_in,
    out,
    dual_out,
    w_all,
    qn,
    dqn,
    kn,
    dkn,
    q_all,
    dq_all,
    k_all,
    dk_all,
    v_all,
    dv_all,
    attn,
    acc,
    give,
    got,
    w_recv,
    w_send,
    first_sem,
    far_recv,
    far_send,
    kv_recv,
    kv_send,
    q_recv,
    q_send,
    own_sem,
    part_recv,
    part_send,
):
    dp = lax.axis_index("dp")
    seq = lax.axis_index("seq")
    z, y, hi = dp // 8, lax.rem(dp // 2, 4), lax.rem(dp, 2)
    lo, core = seq // 2, lax.rem(seq, 2)
    way = 1 - 2 * core

    def unit(zz, yy, hh):
        return zz * 8 + yy * 2 + hh

    def z_at(off):
        return lax.rem(z + off * way + NZ, NZ)

    def y_at(off):
        return lax.rem(y + off * way + NY, NY)

    side = {
        "zf": (unit(z_at(1), y, hi), seq),
        "zb": (unit(z_at(-1), y, hi), seq),
        "yf": (unit(z, y_at(1), hi), seq),
        "yb": (unit(z, y_at(-1), hi), seq),
        "hi": (unit(z, y, 1 - hi), (1 - lo) * 2 + core),
        "lo": (dp, (1 - lo) * 2 + core),
        "cross": (dp, (1 - lo) * 2 + 1 - core),
        "mate": (dp, lo * 2 + 1 - core),
    }

    barrier = pltpu.get_barrier_semaphore()
    for target in side.values():
        pl.semaphore_signal(barrier, inc=1, device_id=target, device_id_type=MESH)
    pl.semaphore_wait(barrier, len(side))

    def remote(src, dst, send_sem, recv_sem, to):
        return pltpu.make_async_remote_copy(
            src_ref=src,
            dst_ref=dst,
            send_sem=send_sem,
            recv_sem=recv_sem,
            device_id=side[to],
            device_id_type=MESH,
        )

    own_w = pltpu.make_async_copy(w_in, w_all.at[lo, dp], first_sem.at[0])
    lo_w = remote(w_in, w_all.at[lo, dp], first_sem.at[1], first_sem.at[2], "lo")

    def piece(stream, source, flip):
        if stream == 0:
            return w_all.at[:, source, pl.ds(0, 32), :]
        block = lo if (stream == 1) != flip else 1 - lo
        return w_all.at[block, source, pl.ds(32, 48), :]

    def w_copy(stream, source, flip, to):
        where = piece(stream, source, flip)
        return remote(where, where, w_send.at[stream], w_recv.at[stream, source], to)

    def own_part(from_input, to):
        block = lo if from_input else 1 - lo
        held = w_in if from_input else w_all.at[block, dp]
        for rows, stream in ((pl.ds(0, 32), 0), (pl.ds(32, 48), 1 if from_input else 2)):
            remote(
                held.at[rows, :],
                w_all.at[block, dp, rows, :],
                w_send.at[stream],
                w_recv.at[stream, dp],
                to,
            ).start()

    lo_w.start()
    for to in ("hi", "yf", "yb", "zf", "zb"):
        own_part(True, to)
    own_w.start()

    def second():
        own_w.wait()
        lo_w.wait_recv()
        for to in ("hi", "yf", "yb", "zf", "zb"):
            own_part(False, to)

    def src(zo, yo, flip):
        return unit(z_at(-zo), y_at(-yo), 1 - hi if flip else hi)

    def z_next(zo):
        if zo == 0:
            return ("zf", "zb")
        if zo > 0:
            return ("zf",) if zo < 4 else ()
        return ("zb",) if zo > -3 else ()

    y_next = {0: ("yf", "yb"), 1: ("yf",), -1: (), 2: ()}

    def w_targets(stream, zo, yo, flip):
        if stream == 0:
            if flip:
                return ()
            return (z_next(zo) if yo == 0 else ()) + y_next[yo] + ("hi",)
        if stream == 1:
            return (y_next[yo] if zo == 0 else ()) + z_next(zo)
        return (z_next(zo) if yo == 0 else ()) + y_next[yo]

    def arrive(stream, zo, yo, flip):
        source = src(zo, yo, flip)
        w_copy(stream, source, flip, "zf").wait_recv()
        for to in w_targets(stream, zo, yo, flip):
            w_copy(stream, source, flip, to).start()

    def mine(group):
        return core + 2 * group

    def theirs(group):
        return 1 - core + 2 * group

    kv_home = (k_all, dk_all, v_all, dv_all)
    whole = pl.ds(0, BLK)

    def kv_source(tensor, block, cols):
        if tensor < 2:
            return (kn, dkn)[tensor].at[block, :, cols]
        first = pl.multiple_of(block * BLK + cols.start, 128)
        return (v_in if tensor == 2 else dv_in).at[:, pl.ds(first, cols.size)]

    def kv_far(head, tensor, which):
        group, cols = head // 5, pl.ds(head % 5 * HDIM, HDIM)
        return remote(
            kv_source(tensor, theirs(group) if which else mine(group), cols),
            kv_home[tensor].at[group, pl.ds((2 + which) * ROWS, ROWS), cols],
            far_send.at[which],
            far_recv.at[head, which],
            ("lo", "cross")[which],
        )

    def kv_mate(group, tensor):
        return remote(
            kv_source(tensor, theirs(group), whole),
            kv_home[tensor].at[group, pl.ds(ROWS, ROWS), :],
            kv_send.at[group, tensor],
            kv_recv.at[group, tensor],
            "mate",
        )

    def kv_own(group, tensor):
        return pltpu.make_async_copy(
            kv_source(tensor, mine(group), whole),
            kv_home[tensor].at[group, pl.ds(0, ROWS), :],
            own_sem.at[group, tensor],
        )

    q_from, q_home = (qn, dqn), (q_all, dq_all)

    def q_copy(group, tensor):
        return remote(
            q_from[tensor].at[theirs(group)],
            q_home[tensor].at[group, pl.ds(ROWS, ROWS), :],
            q_send.at[group, tensor],
            q_recv.at[group, tensor],
            "mate",
        )

    def q_own(group, tensor):
        return pltpu.make_async_copy(
            q_from[tensor].at[mine(group)],
            q_home[tensor].at[group, pl.ds(0, ROWS), :],
            own_sem.at[group, 4 + tensor],
        )

    def send_far(head):
        for tensor in (2, 3, 0, 1):
            for which in range(2):
                kv_far(head, tensor, which).start()

    def start_keys():
        for head in range(4):
            send_far(head)
        for group in range(2):
            for tensor in range(4):
                kv_mate(group, tensor).start()
                kv_own(group, tensor).start()

    def start_queries():
        for group in range(2):
            for tensor in range(2):
                q_copy(group, tensor).start()
                q_own(group, tensor).start()

    def wait_group(group):
        for tensor in range(4):
            kv_own(group, tensor).wait()
            kv_mate(group, tensor).wait_recv()
        for tensor in range(2):
            q_own(group, tensor).wait()
            q_copy(group, tensor).wait_recv()

    factor = HDIM ** (-0.5)
    nt = (((1,), (1,)), ((), ()))

    def head(number):
        if number + 4 < 10:
            send_far(number + 4)
        group, cols = number // 5, pl.ds(number % 5 * HDIM, HDIM)
        if number % 5 == 0:
            wait_group(group)
        for which in range(2):
            four = k_all.at[group, :, cols]
            pltpu.make_async_copy(four, four, far_recv.at[number, which]).wait()
        queries, dual_queries = q_all[group, :, cols], dq_all[group, :, cols]
        keys, dual_keys = k_all[group, :, cols], dk_all[group, :, cols]
        values, dual_values = v_all[group, :, cols], dv_all[group, :, cols]
        scores = lax.dot_general(queries, keys, nt, preferred_element_type=F32) * factor
        dual_scores = (
            lax.dot_general(
                jnp.concatenate([dual_queries, queries], axis=1),
                jnp.concatenate([keys, dual_keys], axis=1),
                nt,
                preferred_element_type=F32,
            )
            * factor
        )
        raised = jnp.exp(scores - jnp.max(scores, axis=-1, keepdims=True))
        probs = raised * (1.0 / jnp.sum(raised, axis=-1, keepdims=True))
        spread = probs * (dual_scores - jnp.sum(probs * dual_scores, axis=-1, keepdims=True))
        low = probs.astype(BF16)
        both = jnp.dot(
            low, jnp.concatenate([values, dual_values], axis=1), preferred_element_type=F32
        )
        dual = both[:, HDIM:] + jnp.dot(spread.astype(BF16), values, preferred_element_type=F32)
        plain = both[:, :HDIM].astype(BF16)
        dual = dual.astype(BF16)
        for owner in range(2):
            rows = slice(owner * ROWS, (owner + 1) * ROWS)
            attn[group, pl.ds(owner * 256, ROWS), cols] = plain[rows]
            attn[group, pl.ds(owner * 256 + ROWS, ROWS), cols] = dual[rows]

    def plane_of(index):
        return z_at(-Z_OFFS[index])

    def product(group, plane, low=0, high=BLK):
        first = pl.multiple_of(plane * 8, 8)
        cols = pl.ds(low, high - low)
        weight = w_all[group, pl.ds(first, 8), :, cols].reshape(PLANE, high - low)
        return lax.dot_general(attn[group, :, cols], weight, nt, preferred_element_type=F32)

    def part_copy(plane, index):
        return remote(
            give.at[index], got.at[plane], part_send.at[index], part_recv.at[plane], "mate"
        )

    def hand_over(index, total):
        acc[index, pl.ds(0, 256), :] = total[:256]
        give[index] = total[256:].astype(BF16)
        part_copy(plane_of(index), index).start()

    def project(kind, index):
        plane = plane_of(index)
        if kind == FIRST:
            acc[index] = product(0, plane)
        elif kind == MIDDLE:
            acc[index] += product(1, plane, 0, 384)
        elif kind == LAST:
            hand_over(index, acc[index] + product(1, plane, 384, BLK))
        elif kind == REST:
            hand_over(index, acc[index] + product(1, plane))
        else:
            hand_over(index, product(0, plane) + product(1, plane))

    def finish(index):
        plane = plane_of(index)
        part_copy(plane, index).wait_recv()
        total = (acc[index, pl.ds(0, 256), :] + got[plane].astype(F32)).astype(BF16)
        cols = pl.ds(pl.multiple_of(plane * PLANE, 128), PLANE)
        out[:, cols] = total[:ROWS]
        dual_out[:, cols] = total[ROWS:]

    for item in ORDER:
        if item < SECOND:
            stream, rest = divmod(item, 64)
            zo, rest = divmod(rest, 8)
            yo, flip = divmod(rest, 2)
            arrive(stream, Z_OFFS[zo], Y_OFFS[yo], flip == 1)
        elif item == SECOND:
            second()
        elif item == KEY_NORM:
            rms_tangent(k_in, dk_in, k_gain, kn, dkn)
        elif item == KEYS:
            start_keys()
        elif item == QUERY_NORM:
            rms_tangent(q_in, dq_in, q_gain, qn, dqn)
        elif item == QUERIES:
            start_queries()
        elif item < FIRST:
            head(item - HEAD)
        elif item < FINISH:
            project(item // 10 * 10, item % 10)
        else:
            finish(item - FINISH)

    lo_w.wait_send()
    for which in range(2):
        pltpu.make_async_copy(k_all, k_all, far_send.at[which]).wait()
    for group in range(2):
        for tensor in range(4):
            kv_mate(group, tensor).wait_send()
        for tensor in range(2):
            q_copy(group, tensor).wait_send()
    sent = (w_all.at[:, pl.ds(0, 63), pl.ds(0, 32), :],) + tuple(
        w_all.at[j, pl.ds(0, 63), pl.ds(32, 48), :] for j in range(2)
    )
    for stream in range(3):
        pltpu.make_async_copy(sent[stream], sent[stream], w_send.at[stream]).wait()
    for index in range(8):
        part_copy(plane_of(index), index).wait_send()


def body(q, k, v, dq, dk, dv, q_gain, k_gain, weight):
    rows, width = q.shape
    vmem = pl.BlockSpec(memory_space=pltpu.VMEM)
    hbm = pl.BlockSpec(memory_space=pl.ANY)
    sem = pltpu.SemaphoreType.DMA
    kv = pltpu.VMEM((2, 4 * ROWS, BLK), BF16)
    qs = pltpu.VMEM((2, 2 * ROWS, BLK), BF16)
    normed = pltpu.VMEM((4, ROWS, BLK), BF16)
    shape = jax.ShapeDtypeStruct((rows, 2 * width), BF16)
    return pl.pallas_call(
        kernel,
        out_shape=(shape, shape),
        in_specs=[vmem] * 4 + [hbm] * 2 + [vmem] * 2 + [hbm],
        out_specs=(vmem, vmem),
        scratch_shapes=[
            pltpu.VMEM((2, 64, UNIT, BLK), BF16),
            normed,
            normed,
            normed,
            normed,
            qs,
            qs,
            kv,
            kv,
            kv,
            kv,
            pltpu.VMEM((2, 4 * ROWS, BLK), BF16),
            pltpu.VMEM((8, 4 * ROWS, PLANE), F32),
            pltpu.VMEM((8, 2 * ROWS, PLANE), BF16),
            pltpu.VMEM((8, 2 * ROWS, PLANE), BF16),
            sem((3, 64)),
            sem((3,)),
            sem((3,)),
            sem((10, 2)),
            sem((2,)),
            sem((2, 4)),
            sem((2, 4)),
            sem((2, 2)),
            sem((2, 2)),
            sem((2, 6)),
            sem((8,)),
            sem((8,)),
        ],
        compiler_params=pltpu.CompilerParams(
            collective_id=0, has_side_effects=True, vmem_limit_bytes=60 * 1024 * 1024
        ),
        name="tangent_attention",
    )(q, dq, k, dk, v, dv, q_gain, k_gain, weight.T)


def solution(mesh):
    tokens = P(("dp", "seq"), None)
    return jax.shard_map(
        body,
        mesh=mesh,
        in_specs=(tokens,) * 6 + (P(), P(), P("seq", "dp")),
        out_specs=(tokens, tokens),
        check_vma=False,
    )
```

```python
import jax
import jax.numpy as jnp
from jax import lax
from jax.experimental import pallas as pl
from jax.experimental.pallas import tpu as pltpu
from jax.sharding import PartitionSpec as P

HDIM = 128
NZ, NY = 8, 4
ROWS = 128
BLK = 640
UNIT = 80
PLANE = 640
EPS = 1e-06
MESH = pl.DeviceIdType.MESH
BF16 = jnp.bfloat16
F32 = jnp.float32

Z_OFFS = (0, 1, -1, 2, -2, 3, -3, 4)
Y_OFFS = (0, 1, -1, 2)
SECOND, KEY_NORM, KEYS, QUERY_NORM, QUERIES, HEAD = 400, 401, 402, 403, 404, 500
FIRST, MIDDLE, LAST, REST, WHOLE = 600, 610, 620, 630, 640
STREAMS = (
    (0, 32, True, "zyh"),
    (0, 32, False, "zyh"),
    (32, 48, True, "hyz"),
    (32, 48, False, "hzy"),
)
ORDER = (
    401, 402, 8, 16, 2, 4, 1, 400, 136, 144, 130, 132, 129, 403, 404, 24, 10, 12, 32, 9, 18, 20, 72,
    80, 17, 6, 68, 3, 200, 208, 66, 196, 5, 500, 152, 160, 194, 133, 65, 138, 146, 134, 28, 193, 36,
    25, 140, 148, 131, 76, 11, 26, 137, 145, 84, 13, 14, 40, 48, 33, 34, 204, 501, 88, 96, 22, 19,
    212, 21, 216, 224, 74, 73, 82, 197, 168, 176, 81, 44, 202, 7, 141, 149, 52, 69, 210, 92, 154,
    162, 67, 502, 70, 100, 29, 142, 150, 198, 220, 37, 201, 209, 77, 195, 228, 27, 135, 156, 164,
    30, 85, 42, 50, 139, 147, 15, 503, 38, 41, 153, 161, 90, 205, 49, 56, 112, 98, 35, 213, 104,
    218, 240, 89, 226, 232, 78, 97, 165, 86, 23, 184, 60, 504, 206, 116, 178, 75, 157, 83, 214, 166,
    108, 45, 170, 203, 225, 53, 244, 158, 93, 211, 151, 236, 71, 199, 600, 217, 46, 180, 101, 505,
    54, 143, 31, 163, 94, 229, 43, 58, 172, 114, 177, 51, 102, 155, 39, 106, 181, 221, 91, 222, 169,
    182, 242, 57, 120, 506, 230, 241, 234, 113, 248, 99, 207, 167, 105, 227, 173, 79, 601, 124, 215,
    179, 186, 87, 602, 174, 219, 61, 245, 233, 62, 507, 118, 159, 117, 183, 252, 109, 610, 110, 188,
    611, 246, 47, 171, 612, 122, 55, 185, 189, 243, 95, 237, 190, 238, 59, 249, 250, 115, 175, 231,
    508, 103, 187, 223, 603, 613, 235, 126, 107, 604, 121, 614, 247, 125, 253, 191, 251, 63, 254,
    119, 606, 239, 616, 111, 509, 620, 123, 621, 255, 127, 622, 623, 624, 645, 626, 647,
)


def rms_tangent(primal_ref, tangent_ref, gain_ref, normed_ref, dual_ref):
    width = primal_ref.shape[1]
    for row in range(0, ROWS, 32):
        rows = pl.ds(row, 32)
        primal = primal_ref[rows, :].astype(F32)
        tangent = tangent_ref[rows, :].astype(F32)
        inverse = lax.rsqrt(jnp.sum(primal * primal, axis=-1, keepdims=True) * (1.0 / width) + EPS)
        across = jnp.sum(primal * tangent, axis=-1, keepdims=True) * (1.0 / width)
        pull = inverse * inverse * inverse * across
        gain = gain_ref[...].reshape(1, width)
        normed = (primal * inverse * gain).astype(BF16)
        dual = (gain * (tangent * inverse - primal * pull)).astype(BF16)
        for block in range(4):
            normed_ref[block, rows, :] = normed[:, block * BLK : (block + 1) * BLK]
            dual_ref[block, rows, :] = dual[:, block * BLK : (block + 1) * BLK]


def kernel(
    q_in,
    dq_in,
    k_in,
    dk_in,
    v_in,
    dv_in,
    q_gain,
    k_gain,
    w_in,
    out,
    dual_out,
    got,
    dual_got,
    w_all,
    qn,
    dqn,
    kn,
    dkn,
    q_all,
    dq_all,
    k_all,
    dk_all,
    v_all,
    dv_all,
    attn,
    acc,
    give,
    keep,
    w_recv,
    w_send,
    first_sem,
    far_recv,
    far_send,
    kv_recv,
    kv_send,
    q_recv,
    q_send,
    own_sem,
    part_recv,
    part_send,
    out_sem,
):
    dp = lax.axis_index("dp")
    seq = lax.axis_index("seq")
    z, y, hi = dp // 8, lax.rem(dp // 2, 4), lax.rem(dp, 2)
    lo, core = seq // 2, lax.rem(seq, 2)
    way = 1 - 2 * core

    def unit(zz, yy, hh):
        return zz * 8 + yy * 2 + hh

    def z_at(off):
        return lax.rem(z + off * way + NZ, NZ)

    def y_at(off):
        return lax.rem(y + off * way + NY, NY)

    side = {
        "zf": (unit(z_at(1), y, hi), seq),
        "zb": (unit(z_at(-1), y, hi), seq),
        "yf": (unit(z, y_at(1), hi), seq),
        "yb": (unit(z, y_at(-1), hi), seq),
        "hi": (unit(z, y, 1 - hi), (1 - lo) * 2 + core),
        "lo": (dp, (1 - lo) * 2 + core),
        "cross": (dp, (1 - lo) * 2 + 1 - core),
        "mate": (dp, lo * 2 + 1 - core),
    }

    barrier = pltpu.get_barrier_semaphore()
    for target in side.values():
        pl.semaphore_signal(barrier, inc=1, device_id=target, device_id_type=MESH)
    pl.semaphore_wait(barrier, len(side))

    def remote(src, dst, send_sem, recv_sem, to):
        return pltpu.make_async_remote_copy(
            src_ref=src,
            dst_ref=dst,
            send_sem=send_sem,
            recv_sem=recv_sem,
            device_id=side[to],
            device_id_type=MESH,
        )

    own_w = pltpu.make_async_copy(w_in, w_all.at[lo, dp], first_sem.at[0])
    lo_w = remote(w_in, w_all.at[lo, dp], first_sem.at[1], first_sem.at[2], "lo")

    def piece(stream, source, flip):
        first, count, began, _ = STREAMS[stream]
        block = lo if began != flip else 1 - lo
        return w_all.at[block, source, pl.ds(first, count), :]

    def w_copy(stream, source, flip, to):
        where = piece(stream, source, flip)
        return remote(where, where, w_send.at[stream], w_recv.at[stream, source], to)

    def own_part(began, to):
        for stream, (first, count, from_input, _) in enumerate(STREAMS):
            if from_input != began:
                continue
            where = piece(stream, dp, False)
            held = w_in.at[pl.ds(first, count), :] if began else where
            remote(held, where, w_send.at[stream], w_recv.at[stream, dp], to).start()

    lo_w.start()
    for to in ("hi", "yf", "yb", "zf", "zb"):
        own_part(True, to)
    own_w.start()

    def second():
        own_w.wait()
        lo_w.wait_recv()
        for to in ("hi", "yf", "yb", "zf", "zb"):
            own_part(False, to)

    def src(zo, yo, flip):
        return unit(z_at(-zo), y_at(-yo), 1 - hi if flip else hi)

    def z_next(zo):
        if zo == 0:
            return ("zf", "zb")
        if zo > 0:
            return ("zf",) if zo < 4 else ()
        return ("zb",) if zo > -3 else ()

    y_next = {0: ("yf", "yb"), 1: ("yf",), -1: (), 2: ()}

    def w_targets(stream, zo, yo, flip):
        axes = STREAMS[stream][3]
        if axes == "zyh":
            if flip:
                return ()
            return (z_next(zo) if yo == 0 else ()) + y_next[yo] + ("hi",)
        if axes == "hyz":
            return (y_next[yo] if zo == 0 else ()) + z_next(zo)
        return (z_next(zo) if yo == 0 else ()) + y_next[yo]

    def arrive(stream, zo, yo, flip):
        source = src(zo, yo, flip)
        w_copy(stream, source, flip, "zf").wait_recv()
        for to in w_targets(stream, zo, yo, flip):
            w_copy(stream, source, flip, to).start()

    def mine(group):
        return core + 2 * group

    def theirs(group):
        return 1 - core + 2 * group

    kv_home = (k_all, dk_all, v_all, dv_all)
    whole = pl.ds(0, BLK)

    def kv_source(tensor, block, cols):
        if tensor < 2:
            return (kn, dkn)[tensor].at[block, :, cols]
        first = pl.multiple_of(block * BLK + cols.start, 128)
        return (v_in if tensor == 2 else dv_in).at[:, pl.ds(first, cols.size)]

    def kv_far(head, tensor, which):
        group, cols = head // 5, pl.ds(head % 5 * HDIM, HDIM)
        return remote(
            kv_source(tensor, theirs(group) if which else mine(group), cols),
            kv_home[tensor].at[group, pl.ds((2 + which) * ROWS, ROWS), cols],
            far_send.at[which],
            far_recv.at[head, which],
            ("lo", "cross")[which],
        )

    def kv_mate(group, tensor):
        return remote(
            kv_source(tensor, theirs(group), whole),
            kv_home[tensor].at[group, pl.ds(ROWS, ROWS), :],
            kv_send.at[group, tensor],
            kv_recv.at[group, tensor],
            "mate",
        )

    def kv_own(group, tensor):
        return pltpu.make_async_copy(
            kv_source(tensor, mine(group), whole),
            kv_home[tensor].at[group, pl.ds(0, ROWS), :],
            own_sem.at[group, tensor],
        )

    q_from, q_home = (qn, dqn), (q_all, dq_all)

    def q_copy(group, tensor):
        return remote(
            q_from[tensor].at[theirs(group)],
            q_home[tensor].at[group, pl.ds(ROWS, ROWS), :],
            q_send.at[group, tensor],
            q_recv.at[group, tensor],
            "mate",
        )

    def q_own(group, tensor):
        return pltpu.make_async_copy(
            q_from[tensor].at[mine(group)],
            q_home[tensor].at[group, pl.ds(0, ROWS), :],
            own_sem.at[group, 4 + tensor],
        )

    def send_far(head):
        for tensor in (2, 3, 0, 1):
            for which in range(2):
                kv_far(head, tensor, which).start()

    def start_keys():
        for head in range(4):
            send_far(head)
        for group in range(2):
            for tensor in range(4):
                kv_mate(group, tensor).start()
                kv_own(group, tensor).start()

    def start_queries():
        for group in range(2):
            for tensor in range(2):
                q_copy(group, tensor).start()
                q_own(group, tensor).start()

    def wait_group(group):
        for tensor in range(4):
            kv_own(group, tensor).wait()
            kv_mate(group, tensor).wait_recv()
        for tensor in range(2):
            q_own(group, tensor).wait()
            q_copy(group, tensor).wait_recv()

    factor = HDIM ** (-0.5)
    nt = (((1,), (1,)), ((), ()))

    def head(number):
        if number + 4 < 10:
            send_far(number + 4)
        group, cols = number // 5, pl.ds(number % 5 * HDIM, HDIM)
        if number % 5 == 0:
            wait_group(group)
        for which in range(2):
            four = k_all.at[group, :, cols]
            pltpu.make_async_copy(four, four, far_recv.at[number, which]).wait()
        queries, dual_queries = q_all[group, :, cols], dq_all[group, :, cols]
        keys, dual_keys = k_all[group, :, cols], dk_all[group, :, cols]
        values, dual_values = v_all[group, :, cols], dv_all[group, :, cols]
        scores = lax.dot_general(queries, keys, nt, preferred_element_type=F32) * factor
        dual_scores = (
            lax.dot_general(
                jnp.concatenate([dual_queries, queries], axis=1),
                jnp.concatenate([keys, dual_keys], axis=1),
                nt,
                preferred_element_type=F32,
            )
            * factor
        )
        raised = jnp.exp(scores - jnp.max(scores, axis=-1, keepdims=True))
        probs = raised * (1.0 / jnp.sum(raised, axis=-1, keepdims=True))
        spread = probs * (dual_scores - jnp.sum(probs * dual_scores, axis=-1, keepdims=True))
        low = probs.astype(BF16)
        both = jnp.dot(
            low, jnp.concatenate([values, dual_values], axis=1), preferred_element_type=F32
        )
        dual = both[:, HDIM:] + jnp.dot(spread.astype(BF16), values, preferred_element_type=F32)
        plain = both[:, :HDIM].astype(BF16)
        dual = dual.astype(BF16)
        for owner in range(2):
            rows = slice(owner * ROWS, (owner + 1) * ROWS)
            attn[group, pl.ds(owner * 256, ROWS), cols] = plain[rows]
            attn[group, pl.ds(owner * 256 + ROWS, ROWS), cols] = dual[rows]

    def plane_of(index):
        return z_at(-Z_OFFS[index])

    def product(group, plane, low=0, high=BLK):
        first = pl.multiple_of(plane * 8, 8)
        cols = pl.ds(low, high - low)
        weight = w_all[group, pl.ds(first, 8), :, cols].reshape(PLANE, high - low)
        return lax.dot_general(attn[group, :, cols], weight, nt, preferred_element_type=F32)

    def out_copies(index):
        first = pl.multiple_of(plane_of(index) * PLANE, 128)
        cols = pl.ds(first, PLANE)
        copies = []
        for half in range(2):
            rows = pl.ds(half * ROWS, ROWS)
            copies.append(
                remote(
                    give.at[index, rows, :],
                    (got, dual_got)[half].at[:, cols],
                    part_send.at[index, half],
                    part_recv.at[plane_of(index), half],
                    "mate",
                )
            )
            copies.append(
                pltpu.make_async_copy(
                    keep.at[index, rows, :], (out, dual_out)[half].at[:, cols], out_sem.at[index, half]
                )
            )
        return copies

    def hand_over(index, total):
        give[index] = total[256:].astype(BF16)
        keep[index] = total[:256].astype(BF16)
        for copy in out_copies(index):
            copy.start()

    def project(kind, index):
        plane = plane_of(index)
        if kind == FIRST:
            acc[index] = product(0, plane)
        elif kind == MIDDLE:
            acc[index] += product(1, plane, 0, 384)
        elif kind == LAST:
            hand_over(index, acc[index] + product(1, plane, 384, BLK))
        elif kind == REST:
            hand_over(index, acc[index] + product(1, plane))
        else:
            hand_over(index, product(0, plane) + product(1, plane))

    for item in ORDER:
        if item < SECOND:
            stream, rest = divmod(item, 64)
            zo, rest = divmod(rest, 8)
            yo, flip = divmod(rest, 2)
            arrive(stream, Z_OFFS[zo], Y_OFFS[yo], flip == 1)
        elif item == SECOND:
            second()
        elif item == KEY_NORM:
            rms_tangent(k_in, dk_in, k_gain, kn, dkn)
        elif item == KEYS:
            start_keys()
        elif item == QUERY_NORM:
            rms_tangent(q_in, dq_in, q_gain, qn, dqn)
        elif item == QUERIES:
            start_queries()
        elif item < FIRST:
            head(item - HEAD)
        else:
            project(item // 10 * 10, item % 10)

    lo_w.wait_send()
    for which in range(2):
        pltpu.make_async_copy(k_all, k_all, far_send.at[which]).wait()
    for group in range(2):
        for tensor in range(4):
            kv_mate(group, tensor).wait_send()
        for tensor in range(2):
            q_copy(group, tensor).wait_send()
    for stream, (first, count, _, _) in enumerate(STREAMS):
        sent = w_all.at[0, pl.ds(0, 63), pl.ds(first, count), :]
        pltpu.make_async_copy(sent, sent, w_send.at[stream]).wait()
    for index in range(8):
        for copy in out_copies(index):
            copy.wait()


def body(q, k, v, dq, dk, dv, q_gain, k_gain, weight):
    rows, width = q.shape
    vmem = pl.BlockSpec(memory_space=pltpu.VMEM)
    hbm = pl.BlockSpec(memory_space=pl.ANY)
    sem = pltpu.SemaphoreType.DMA
    kv = pltpu.VMEM((2, 4 * ROWS, BLK), BF16)
    qs = pltpu.VMEM((2, 2 * ROWS, BLK), BF16)
    normed = pltpu.VMEM((4, ROWS, BLK), BF16)
    shape = jax.ShapeDtypeStruct((rows, 2 * width), BF16)
    plain, dual, got, dual_got = pl.pallas_call(
        kernel,
        out_shape=(shape,) * 4,
        in_specs=[vmem] * 4 + [hbm] * 2 + [vmem] * 2 + [hbm],
        out_specs=(hbm,) * 4,
        scratch_shapes=[
            pltpu.VMEM((2, 64, UNIT, BLK), BF16),
            normed,
            normed,
            normed,
            normed,
            qs,
            qs,
            kv,
            kv,
            kv,
            kv,
            pltpu.VMEM((2, 4 * ROWS, BLK), BF16),
            pltpu.VMEM((8, 4 * ROWS, PLANE), F32),
            pltpu.VMEM((8, 2 * ROWS, PLANE), BF16),
            pltpu.VMEM((8, 2 * ROWS, PLANE), BF16),
            sem((4, 64)),
            sem((4,)),
            sem((3,)),
            sem((10, 2)),
            sem((2,)),
            sem((2, 4)),
            sem((2, 4)),
            sem((2, 2)),
            sem((2, 2)),
            sem((2, 6)),
            sem((8, 2)),
            sem((8, 2)),
            sem((8, 2)),
        ],
        compiler_params=pltpu.CompilerParams(
            collective_id=0, has_side_effects=True, vmem_limit_bytes=60 * 1024 * 1024
        ),
        name="tangent_attention",
    )(q, dq, k, dk, v, dv, q_gain, k_gain, weight.T)
    return (
        (plain.astype(F32) + got.astype(F32)).astype(BF16),
        (dual.astype(F32) + dual_got.astype(F32)).astype(BF16),
    )


def solution(mesh):
    tokens = P(("dp", "seq"), None)
    return jax.shard_map(
        body,
        mesh=mesh,
        in_specs=(tokens,) * 6 + (P(), P(), P("seq", "dp")),
        out_specs=(tokens, tokens),
        check_vma=False,
    )
```

```python
import jax
import jax.numpy as jnp
from jax import lax
from jax.experimental import pallas as pl
from jax.experimental.pallas import tpu as pltpu
from jax.sharding import PartitionSpec as P

HDIM = 128
NZ, NY = 8, 4
ROWS = 128
BLK = 640
UNIT = 80
PLANE = 640
EPS = 1e-06
MESH = pl.DeviceIdType.MESH
BF16 = jnp.bfloat16
F32 = jnp.float32

Z_OFFS = (0, 1, -1, 2, -2, 3, -3, 4)
Y_OFFS = (0, 1, -1, 2)
SECOND, KEY_NORM, KEYS, QUERY_NORM, QUERIES, HEAD = 400, 401, 402, 403, 404, 500
FIRST, MIDDLE, LAST, REST, WHOLE = 600, 610, 620, 630, 640
STREAMS = (
    (0, 32, True, "zyh"),
    (0, 32, False, "zyh"),
    (32, 48, True, "hyz"),
    (32, 48, False, "hzy"),
)
ORDER = (
    401, 402, 8, 16, 2, 4, 1, 400, 136, 144, 130, 132, 129, 403, 404, 24, 10, 12, 32, 9, 18, 20, 72,
    80, 17, 6, 68, 3, 200, 208, 66, 196, 5, 500, 152, 160, 194, 133, 65, 138, 146, 134, 28, 193, 36,
    25, 140, 148, 131, 76, 11, 26, 137, 145, 84, 13, 14, 40, 48, 33, 34, 204, 501, 88, 96, 22, 19,
    212, 21, 216, 224, 74, 73, 82, 197, 168, 176, 81, 44, 202, 7, 141, 149, 52, 69, 210, 92, 154,
    162, 67, 502, 70, 100, 29, 142, 150, 198, 220, 37, 201, 209, 77, 195, 228, 27, 135, 156, 164,
    30, 85, 42, 50, 139, 147, 15, 503, 38, 41, 153, 161, 90, 205, 49, 56, 112, 98, 35, 213, 104,
    218, 240, 89, 226, 232, 78, 97, 165, 86, 23, 184, 60, 504, 206, 116, 178, 75, 157, 83, 214, 166,
    108, 45, 170, 203, 225, 53, 244, 158, 93, 211, 151, 236, 71, 199, 600, 217, 46, 180, 101, 505,
    54, 143, 31, 163, 94, 229, 43, 58, 172, 114, 177, 51, 102, 155, 39, 106, 181, 221, 91, 222, 169,
    182, 242, 57, 120, 506, 230, 241, 234, 113, 248, 99, 207, 167, 105, 227, 173, 79, 601, 124, 215,
    179, 186, 87, 602, 174, 219, 61, 245, 233, 62, 507, 118, 159, 117, 183, 252, 109, 610, 110, 188,
    611, 246, 47, 171, 612, 122, 55, 185, 189, 243, 95, 237, 190, 238, 59, 249, 250, 115, 175, 231,
    508, 103, 187, 223, 603, 613, 235, 126, 107, 604, 121, 614, 247, 125, 253, 191, 251, 63, 254,
    119, 606, 239, 616, 111, 509, 620, 123, 621, 255, 127, 622, 623, 624, 645, 626, 647,
)


def rms_tangent(primal_ref, tangent_ref, gain_ref, normed_ref, dual_ref):
    width = primal_ref.shape[1]
    for row in range(0, ROWS, 32):
        rows = pl.ds(row, 32)
        primal = primal_ref[rows, :].astype(F32)
        tangent = tangent_ref[rows, :].astype(F32)
        inverse = lax.rsqrt(jnp.sum(primal * primal, axis=-1, keepdims=True) * (1.0 / width) + EPS)
        across = jnp.sum(primal * tangent, axis=-1, keepdims=True) * (1.0 / width)
        pull = inverse * inverse * inverse * across
        gain = gain_ref[...].reshape(1, width)
        normed = (primal * inverse * gain).astype(BF16)
        dual = (gain * (tangent * inverse - primal * pull)).astype(BF16)
        for block in range(4):
            normed_ref[block, rows, :] = normed[:, block * BLK : (block + 1) * BLK]
            dual_ref[block, rows, :] = dual[:, block * BLK : (block + 1) * BLK]


def kernel(
    q_in,
    dq_in,
    k_in,
    dk_in,
    v_in,
    dv_in,
    q_gain,
    k_gain,
    w_in,
    out,
    dual_out,
    got,
    dual_got,
    q_raw,
    dq_raw,
    k_raw,
    dk_raw,
    q_scale,
    k_scale,
    w_all,
    qn,
    dqn,
    kn,
    dkn,
    q_all,
    dq_all,
    k_all,
    dk_all,
    v_all,
    dv_all,
    attn,
    acc,
    give,
    keep,
    load_sem,
    w_recv,
    w_send,
    first_sem,
    far_recv,
    far_send,
    kv_recv,
    kv_send,
    q_recv,
    q_send,
    own_sem,
    part_recv,
    part_send,
    out_sem,
):
    def load(which):
        source, home = loads[which]
        return pltpu.make_async_copy(source, home, load_sem.at[which])

    loads = (
        (k_in, k_raw),
        (dk_in, dk_raw),
        (k_gain, k_scale),
        (q_in, q_raw),
        (dq_in, dq_raw),
        (q_gain, q_scale),
    )
    for which in range(6):
        load(which).start()

    dp = lax.axis_index("dp")
    seq = lax.axis_index("seq")
    z, y, hi = dp // 8, lax.rem(dp // 2, 4), lax.rem(dp, 2)
    lo, core = seq // 2, lax.rem(seq, 2)
    way = 1 - 2 * core

    def unit(zz, yy, hh):
        return zz * 8 + yy * 2 + hh

    def z_at(off):
        return lax.rem(z + off * way + NZ, NZ)

    def y_at(off):
        return lax.rem(y + off * way + NY, NY)

    side = {
        "zf": (unit(z_at(1), y, hi), seq),
        "zb": (unit(z_at(-1), y, hi), seq),
        "yf": (unit(z, y_at(1), hi), seq),
        "yb": (unit(z, y_at(-1), hi), seq),
        "hi": (unit(z, y, 1 - hi), (1 - lo) * 2 + core),
        "lo": (dp, (1 - lo) * 2 + core),
        "cross": (dp, (1 - lo) * 2 + 1 - core),
        "mate": (dp, lo * 2 + 1 - core),
    }

    barrier = pltpu.get_barrier_semaphore()
    for target in side.values():
        pl.semaphore_signal(barrier, inc=1, device_id=target, device_id_type=MESH)
    pl.semaphore_wait(barrier, len(side))

    def remote(src, dst, send_sem, recv_sem, to):
        return pltpu.make_async_remote_copy(
            src_ref=src,
            dst_ref=dst,
            send_sem=send_sem,
            recv_sem=recv_sem,
            device_id=side[to],
            device_id_type=MESH,
        )

    own_w = pltpu.make_async_copy(w_in, w_all.at[lo, dp], first_sem.at[0])
    lo_w = remote(w_in, w_all.at[lo, dp], first_sem.at[1], first_sem.at[2], "lo")

    def piece(stream, source, flip):
        first, count, began, _ = STREAMS[stream]
        block = lo if began != flip else 1 - lo
        return w_all.at[block, source, pl.ds(first, count), :]

    def w_copy(stream, source, flip, to):
        where = piece(stream, source, flip)
        return remote(where, where, w_send.at[stream], w_recv.at[stream, source], to)

    def own_part(began, to):
        for stream, (first, count, from_input, _) in enumerate(STREAMS):
            if from_input != began:
                continue
            where = piece(stream, dp, False)
            held = w_in.at[pl.ds(first, count), :] if began else where
            remote(held, where, w_send.at[stream], w_recv.at[stream, dp], to).start()

    lo_w.start()
    for to in ("hi", "yf", "yb", "zf", "zb"):
        own_part(True, to)
    own_w.start()

    def second():
        own_w.wait()
        lo_w.wait_recv()
        for to in ("hi", "yf", "yb", "zf", "zb"):
            own_part(False, to)

    def src(zo, yo, flip):
        return unit(z_at(-zo), y_at(-yo), 1 - hi if flip else hi)

    def z_next(zo):
        if zo == 0:
            return ("zf", "zb")
        if zo > 0:
            return ("zf",) if zo < 4 else ()
        return ("zb",) if zo > -3 else ()

    y_next = {0: ("yf", "yb"), 1: ("yf",), -1: (), 2: ()}

    def w_targets(stream, zo, yo, flip):
        axes = STREAMS[stream][3]
        if axes == "zyh":
            if flip:
                return ()
            return (z_next(zo) if yo == 0 else ()) + y_next[yo] + ("hi",)
        if axes == "hyz":
            return (y_next[yo] if zo == 0 else ()) + z_next(zo)
        return (z_next(zo) if yo == 0 else ()) + y_next[yo]

    def arrive(stream, zo, yo, flip):
        source = src(zo, yo, flip)
        w_copy(stream, source, flip, "zf").wait_recv()
        for to in w_targets(stream, zo, yo, flip):
            w_copy(stream, source, flip, to).start()

    def mine(group):
        return core + 2 * group

    def theirs(group):
        return 1 - core + 2 * group

    kv_home = (k_all, dk_all, v_all, dv_all)
    whole = pl.ds(0, BLK)

    def kv_source(tensor, block, cols):
        if tensor < 2:
            return (kn, dkn)[tensor].at[block, :, cols]
        first = pl.multiple_of(block * BLK + cols.start, 128)
        return (v_in if tensor == 2 else dv_in).at[:, pl.ds(first, cols.size)]

    def kv_far(head, tensor, which):
        group, cols = head // 5, pl.ds(head % 5 * HDIM, HDIM)
        return remote(
            kv_source(tensor, theirs(group) if which else mine(group), cols),
            kv_home[tensor].at[group, pl.ds((2 + which) * ROWS, ROWS), cols],
            far_send.at[which],
            far_recv.at[head, which],
            ("lo", "cross")[which],
        )

    def kv_mate(group, tensor):
        return remote(
            kv_source(tensor, theirs(group), whole),
            kv_home[tensor].at[group, pl.ds(ROWS, ROWS), :],
            kv_send.at[group, tensor],
            kv_recv.at[group, tensor],
            "mate",
        )

    def kv_own(group, tensor):
        return pltpu.make_async_copy(
            kv_source(tensor, mine(group), whole),
            kv_home[tensor].at[group, pl.ds(0, ROWS), :],
            own_sem.at[group, tensor],
        )

    q_from, q_home = (qn, dqn), (q_all, dq_all)

    def q_copy(group, tensor):
        return remote(
            q_from[tensor].at[theirs(group)],
            q_home[tensor].at[group, pl.ds(ROWS, ROWS), :],
            q_send.at[group, tensor],
            q_recv.at[group, tensor],
            "mate",
        )

    def q_own(group, tensor):
        return pltpu.make_async_copy(
            q_from[tensor].at[mine(group)],
            q_home[tensor].at[group, pl.ds(0, ROWS), :],
            own_sem.at[group, 4 + tensor],
        )

    def send_far(head):
        for tensor in (2, 3, 0, 1):
            for which in range(2):
                kv_far(head, tensor, which).start()

    def start_keys():
        for head in range(4):
            send_far(head)
        for group in range(2):
            for tensor in range(4):
                kv_mate(group, tensor).start()
                kv_own(group, tensor).start()

    def start_queries():
        for group in range(2):
            for tensor in range(2):
                q_copy(group, tensor).start()
                q_own(group, tensor).start()

    def wait_group(group):
        for tensor in range(4):
            kv_own(group, tensor).wait()
            kv_mate(group, tensor).wait_recv()
        for tensor in range(2):
            q_own(group, tensor).wait()
            q_copy(group, tensor).wait_recv()

    factor = HDIM ** (-0.5)
    nt = (((1,), (1,)), ((), ()))

    def head(number):
        if number + 4 < 10:
            send_far(number + 4)
        group, cols = number // 5, pl.ds(number % 5 * HDIM, HDIM)
        if number % 5 == 0:
            wait_group(group)
        for which in range(2):
            four = k_all.at[group, :, cols]
            pltpu.make_async_copy(four, four, far_recv.at[number, which]).wait()
        queries, dual_queries = q_all[group, :, cols], dq_all[group, :, cols]
        keys, dual_keys = k_all[group, :, cols], dk_all[group, :, cols]
        values, dual_values = v_all[group, :, cols], dv_all[group, :, cols]
        scores = lax.dot_general(queries, keys, nt, preferred_element_type=F32) * factor
        dual_scores = (
            lax.dot_general(
                jnp.concatenate([dual_queries, queries], axis=1),
                jnp.concatenate([keys, dual_keys], axis=1),
                nt,
                preferred_element_type=F32,
            )
            * factor
        )
        raised = jnp.exp(scores - jnp.max(scores, axis=-1, keepdims=True))
        probs = raised * (1.0 / jnp.sum(raised, axis=-1, keepdims=True))
        spread = probs * (dual_scores - jnp.sum(probs * dual_scores, axis=-1, keepdims=True))
        low = probs.astype(BF16)
        both = jnp.dot(
            low, jnp.concatenate([values, dual_values], axis=1), preferred_element_type=F32
        )
        dual = both[:, HDIM:] + jnp.dot(spread.astype(BF16), values, preferred_element_type=F32)
        plain = both[:, :HDIM].astype(BF16)
        dual = dual.astype(BF16)
        for owner in range(2):
            rows = slice(owner * ROWS, (owner + 1) * ROWS)
            attn[group, pl.ds(owner * 256, ROWS), cols] = plain[rows]
            attn[group, pl.ds(owner * 256 + ROWS, ROWS), cols] = dual[rows]

    def plane_of(index):
        return z_at(-Z_OFFS[index])

    def product(group, plane, low=0, high=BLK):
        first = pl.multiple_of(plane * 8, 8)
        cols = pl.ds(low, high - low)
        weight = w_all[group, pl.ds(first, 8), :, cols].reshape(PLANE, high - low)
        return lax.dot_general(attn[group, :, cols], weight, nt, preferred_element_type=F32)

    def out_copies(index):
        first = pl.multiple_of(plane_of(index) * PLANE, 128)
        cols = pl.ds(first, PLANE)
        copies = []
        for half in range(2):
            rows = pl.ds(half * ROWS, ROWS)
            copies.append(
                remote(
                    give.at[index, rows, :],
                    (got, dual_got)[half].at[:, cols],
                    part_send.at[index, half],
                    part_recv.at[plane_of(index), half],
                    "mate",
                )
            )
            copies.append(
                pltpu.make_async_copy(
                    keep.at[index, rows, :], (out, dual_out)[half].at[:, cols], out_sem.at[index, half]
                )
            )
        return copies

    def hand_over(index, total):
        give[index] = total[256:].astype(BF16)
        keep[index] = total[:256].astype(BF16)
        for copy in out_copies(index):
            copy.start()

    def project(kind, index):
        plane = plane_of(index)
        if kind == FIRST:
            acc[index] = product(0, plane)
        elif kind == MIDDLE:
            acc[index] += product(1, plane, 0, 384)
        elif kind == LAST:
            hand_over(index, acc[index] + product(1, plane, 384, BLK))
        elif kind == REST:
            hand_over(index, acc[index] + product(1, plane))
        else:
            hand_over(index, product(0, plane) + product(1, plane))

    for item in ORDER:
        if item < SECOND:
            stream, rest = divmod(item, 64)
            zo, rest = divmod(rest, 8)
            yo, flip = divmod(rest, 2)
            arrive(stream, Z_OFFS[zo], Y_OFFS[yo], flip == 1)
        elif item == SECOND:
            second()
        elif item == KEY_NORM:
            for which in range(3):
                load(which).wait()
            rms_tangent(k_raw, dk_raw, k_scale, kn, dkn)
        elif item == KEYS:
            start_keys()
        elif item == QUERY_NORM:
            for which in range(3, 6):
                load(which).wait()
            rms_tangent(q_raw, dq_raw, q_scale, qn, dqn)
        elif item == QUERIES:
            start_queries()
        elif item < FIRST:
            head(item - HEAD)
        else:
            project(item // 10 * 10, item % 10)

    lo_w.wait_send()
    for which in range(2):
        pltpu.make_async_copy(k_all, k_all, far_send.at[which]).wait()
    for group in range(2):
        for tensor in range(4):
            kv_mate(group, tensor).wait_send()
        for tensor in range(2):
            q_copy(group, tensor).wait_send()
    for stream, (first, count, _, _) in enumerate(STREAMS):
        sent = w_all.at[0, pl.ds(0, 63), pl.ds(first, count), :]
        pltpu.make_async_copy(sent, sent, w_send.at[stream]).wait()
    for index in range(8):
        for copy in out_copies(index):
            copy.wait()


def body(q, k, v, dq, dk, dv, q_gain, k_gain, weight):
    rows, width = q.shape
    hbm = pl.BlockSpec(memory_space=pltpu.HBM)
    free = pl.BlockSpec(memory_space=pl.ANY)
    sem = pltpu.SemaphoreType.DMA
    kv = pltpu.VMEM((2, 4 * ROWS, BLK), BF16)
    qs = pltpu.VMEM((2, 2 * ROWS, BLK), BF16)
    normed = pltpu.VMEM((4, ROWS, BLK), BF16)
    raw = pltpu.VMEM((rows, width), BF16)
    scale = pltpu.VMEM((width,), F32)
    shape = jax.ShapeDtypeStruct((rows, 2 * width), BF16)
    plain, dual, got, dual_got = pl.pallas_call(
        kernel,
        out_shape=(shape,) * 4,
        in_specs=[hbm] * 9,
        out_specs=(free,) * 4,
        scratch_shapes=[
            raw,
            raw,
            raw,
            raw,
            scale,
            scale,
            pltpu.VMEM((2, 64, UNIT, BLK), BF16),
            normed,
            normed,
            normed,
            normed,
            qs,
            qs,
            kv,
            kv,
            kv,
            kv,
            pltpu.VMEM((2, 4 * ROWS, BLK), BF16),
            pltpu.VMEM((8, 4 * ROWS, PLANE), F32),
            pltpu.VMEM((8, 2 * ROWS, PLANE), BF16),
            pltpu.VMEM((8, 2 * ROWS, PLANE), BF16),
            sem((6,)),
            sem((4, 64)),
            sem((4,)),
            sem((3,)),
            sem((10, 2)),
            sem((2,)),
            sem((2, 4)),
            sem((2, 4)),
            sem((2, 2)),
            sem((2, 2)),
            sem((2, 6)),
            sem((8, 2)),
            sem((8, 2)),
            sem((8, 2)),
        ],
        compiler_params=pltpu.CompilerParams(
            collective_id=0, has_side_effects=True, vmem_limit_bytes=44 * 1024 * 1024
        ),
        name="tangent_attention",
    )(*(pltpu.with_memory_space_constraint(a, pltpu.HBM) for a in (q, dq, k, dk, v, dv, q_gain, k_gain, weight.T)))
    return (
        (plain.astype(F32) + got.astype(F32)).astype(BF16),
        (dual.astype(F32) + dual_got.astype(F32)).astype(BF16),
    )


def solution(mesh):
    tokens = P(("dp", "seq"), None)
    return jax.shard_map(
        body,
        mesh=mesh,
        in_specs=(tokens,) * 6 + (P(), P(), P("seq", "dp")),
        out_specs=(tokens, tokens),
        check_vma=False,
    )
```

```python
import jax
import jax.numpy as jnp
from jax import lax
from jax.experimental import pallas as pl
from jax.experimental.pallas import tpu as pltpu
from jax.sharding import PartitionSpec as P

HDIM = 128
NZ, NY = 8, 4
ROWS = 128
BLK = 640
UNIT = 80
PLANE = 640
EPS = 1e-06
MESH = pl.DeviceIdType.MESH
BF16 = jnp.bfloat16
F32 = jnp.float32

Z_OFFS = (0, 1, -1, 2, -2, 3, -3, 4)
Y_OFFS = (0, 1, -1, 2)
SECOND, KEY_NORM, KEYS, QUERY_NORM, QUERIES, HEAD = 400, 401, 402, 403, 404, 500
FIRST, MIDDLE, LAST, REST, WHOLE = 600, 610, 620, 630, 640
SEND = 1000
SIDES = ("hi", "yf", "yb", "zf", "zb")
STREAMS = (
    (True, ((0, 32, 0, 512),)),
    (False, ((0, 32, 0, 640),)),
    (True, ((32, 48, 0, 640), (0, 32, 512, 128))),
    (False, ((32, 48, 0, 640),)),
)
PARTS = tuple((stream, part) for stream, (_, parts) in enumerate(STREAMS) for part in parts)
ORDER = (
    1003, 1004, 1641, 1642, 1640, 1643, 1644, 1001, 1002, 1000, 401, 402, 8, 1043, 16, 1084, 1041,
    1042, 1040, 1081, 1082, 1080, 130, 1653, 132, 1654, 1663, 1664, 1651, 129, 136, 400, 144, 2, 4,
    1647, 1960, 1646, 1322, 1320, 1323, 1324, 1321, 1962, 1010, 403, 1963, 1964, 1961, 1020, 404,
    24, 1122, 32, 10, 1123, 12, 1164, 1120, 1162, 1121, 18, 20, 1648, 1160, 1649, 1161, 138, 146,
    1050, 134, 1673, 1060, 1674, 133, 1011, 193, 1967, 1968, 140, 1090, 1969, 148, 68, 1051, 131,
    1100, 72, 1362, 500, 80, 66, 1402, 1363, 1404, 1656, 1340, 1361, 1360, 200, 2002, 208, 28, 2042,
    1401, 194, 1400, 40, 2003, 48, 36, 2044, 1202, 26, 1330, 1201, 34, 1668, 137, 1669, 1242, 145,
    1140, 6, 1241, 1658, 76, 1659, 1200, 14, 1091, 142, 150, 84, 1240, 1203, 501, 135, 201, 2007,
    1966, 1679, 209, 2047, 1331, 1180, 1130, 74, 2008, 2001, 88, 2049, 1442, 96, 1170, 1482, 82,
    1030, 1441, 216, 1443, 44, 42, 224, 1484, 2082, 1380, 1481, 1678, 52, 50, 1070, 2122, 22, 141,
    149, 2124, 1420, 2041, 2083, 502, 195, 139, 147, 1370, 1683, 1724, 1131, 1440, 70, 56, 1282,
    1281, 1734, 92, 1480, 1693, 151, 202, 217, 2087, 1171, 100, 1744, 1410, 2088, 2006, 90, 104,
    225, 1522, 2127, 1220, 1521, 2129, 98, 112, 1562, 1210, 1561, 1523, 143, 1260, 210, 240, 2202,
    1729, 503, 60, 232, 30, 1703, 2046, 2162, 1250, 1110, 1371, 58, 160, 1754, 1350, 1688, 38, 152,
    1411, 1280, 108, 1713, 1749, 162, 1460, 203, 2081, 154, 1500, 106, 1708, 1739, 1211, 164, 116,
    1450, 233, 2167, 2121, 114, 1520, 120, 241, 1602, 1698, 1759, 2207, 504, 211, 1601, 1490, 1251,
    156, 1718, 161, 78, 1804, 1560, 86, 2086, 1300, 153, 2163, 166, 1814, 1451, 218, 2126, 1150, 46,
    1491, 124, 1290, 158, 2168, 165, 1824, 2201, 1190, 2161, 226, 505, 157, 122, 163, 54, 1291,
    1540, 1763, 1809, 1531, 1530, 219, 2166, 1580, 1773, 155, 94, 167, 1834, 1571, 2206, 1570, 227,
    1783, 102, 1611, 1600, 159, 1829, 1971, 242, 1390, 1976, 234, 1768, 248, 2242, 2241, 62, 1819,
    1430, 110, 506, 249, 235, 118, 2247, 1793, 1839, 2246, 1230, 1620, 2011, 243, 168, 1788, 126,
    1610, 2051, 1270, 2016, 170, 1778, 1470, 2056, 2091, 1510, 172, 1798, 2131, 1310, 250, 507, 251,
    169, 1843, 2096, 1550, 2136, 1853, 1590, 2211, 1863, 1, 65, 3, 196, 5, 197, 69, 67, 7, 71, 198,
    199, 174, 2171, 1630, 600, 1848, 610, 173, 1873, 2176, 2216, 171, 1868, 2251, 175, 1858, 2256,
    508, 1878, 9, 11, 13, 204, 73, 205, 77, 15, 75, 79, 206, 207, 601, 611, 17, 19, 21, 212, 81,
    213, 85, 83, 23, 87, 214, 215, 602, 612, 25, 29, 27, 220, 89, 221, 93, 91, 31, 222, 95, 223,
    603, 613, 33, 37, 35, 228, 97, 229, 101, 99, 39, 230, 103, 231, 604, 614, 509, 620, 621, 622,
    623, 624, 41, 45, 43, 236, 237, 105, 109, 107, 47, 111, 238, 239, 645, 49, 53, 51, 244, 245,
    113, 176, 178, 180, 117, 177, 115, 182, 181, 179, 183, 55, 246, 119, 247, 646, 57, 61, 59, 252,
    121, 253, 125, 123, 63, 184, 186, 188, 185, 127, 190, 254, 189, 255, 187, 191, 647,
)


def rms_tangent(primal_ref, tangent_ref, gain_ref, normed_ref, dual_ref):
    width = primal_ref.shape[1]
    for row in range(0, ROWS, 32):
        rows = pl.ds(row, 32)
        primal = primal_ref[rows, :].astype(F32)
        tangent = tangent_ref[rows, :].astype(F32)
        inverse = lax.rsqrt(jnp.sum(primal * primal, axis=-1, keepdims=True) * (1.0 / width) + EPS)
        across = jnp.sum(primal * tangent, axis=-1, keepdims=True) * (1.0 / width)
        pull = inverse * inverse * inverse * across
        gain = gain_ref[...].reshape(1, width)
        normed = (primal * inverse * gain).astype(BF16)
        dual = (gain * (tangent * inverse - primal * pull)).astype(BF16)
        for block in range(4):
            normed_ref[block, rows, :] = normed[:, block * BLK : (block + 1) * BLK]
            dual_ref[block, rows, :] = dual[:, block * BLK : (block + 1) * BLK]


def kernel(
    q_in,
    dq_in,
    k_in,
    dk_in,
    v_in,
    dv_in,
    q_gain,
    k_gain,
    w_in,
    out,
    dual_out,
    got,
    dual_got,
    q_raw,
    dq_raw,
    k_raw,
    dk_raw,
    q_scale,
    k_scale,
    w_all,
    qn,
    dqn,
    kn,
    dkn,
    q_all,
    dq_all,
    k_all,
    dk_all,
    v_all,
    dv_all,
    attn,
    acc,
    give,
    keep,
    load_sem,
    w_recv,
    w_send,
    first_sem,
    far_recv,
    far_send,
    kv_recv,
    kv_send,
    q_recv,
    q_send,
    own_sem,
    part_recv,
    part_send,
    out_sem,
):
    def load(which):
        source, home = loads[which]
        return pltpu.make_async_copy(source, home, load_sem.at[which])

    loads = (
        (k_in, k_raw),
        (dk_in, dk_raw),
        (k_gain, k_scale),
        (q_in, q_raw),
        (dq_in, dq_raw),
        (q_gain, q_scale),
    )
    for which in range(6):
        load(which).start()

    dp = lax.axis_index("dp")
    seq = lax.axis_index("seq")
    z, y, hi = dp // 8, lax.rem(dp // 2, 4), lax.rem(dp, 2)
    lo, core = seq // 2, lax.rem(seq, 2)
    way = 1 - 2 * core

    def unit(zz, yy, hh):
        return zz * 8 + yy * 2 + hh

    def z_at(off):
        return lax.rem(z + off * way + NZ, NZ)

    def y_at(off):
        return lax.rem(y + off * way + NY, NY)

    side = {
        "zf": (unit(z_at(1), y, hi), seq),
        "zb": (unit(z_at(-1), y, hi), seq),
        "yf": (unit(z, y_at(1), hi), seq),
        "yb": (unit(z, y_at(-1), hi), seq),
        "hi": (unit(z, y, 1 - hi), (1 - lo) * 2 + core),
        "lo": (dp, (1 - lo) * 2 + core),
        "cross": (dp, (1 - lo) * 2 + 1 - core),
        "mate": (dp, lo * 2 + 1 - core),
    }

    barrier = pltpu.get_barrier_semaphore()
    for target in side.values():
        pl.semaphore_signal(barrier, inc=1, device_id=target, device_id_type=MESH)
    pl.semaphore_wait(barrier, len(side))

    def remote(src, dst, send_sem, recv_sem, to):
        return pltpu.make_async_remote_copy(
            src_ref=src,
            dst_ref=dst,
            send_sem=send_sem,
            recv_sem=recv_sem,
            device_id=side[to],
            device_id_type=MESH,
        )

    own_w = pltpu.make_async_copy(w_in, w_all.at[lo, dp], first_sem.at[0])
    lo_w = remote(w_in, w_all.at[lo, dp], first_sem.at[1], first_sem.at[2], "lo")

    def src(zo, yo, flip):
        return unit(z_at(-zo), y_at(-yo), 1 - hi if flip else hi)

    def w_copies(code, to):
        stream, rest = divmod(code, 64)
        zo, rest = divmod(rest, 8)
        yo, flip = divmod(rest, 2)
        source = src(Z_OFFS[zo], Y_OFFS[yo], flip)
        began = STREAMS[stream][0]
        block = lo if began != (flip == 1) else 1 - lo
        copies = []
        for index, (owner, (row, rows, col, cols)) in enumerate(PARTS):
            if owner != stream:
                continue
            where = w_all.at[block, source, pl.ds(row, rows), pl.ds(col, cols)]
            held = where
            if began and rest == 0 and zo == 0:
                held = w_in.at[pl.ds(row, rows), pl.ds(col, cols)]
            copies.append(remote(held, where, w_send.at[index], w_recv.at[index, source], to))
        return copies

    lo_w.start()
    own_w.start()

    def second():
        own_w.wait()
        lo_w.wait_recv()

    def mine(group):
        return core + 2 * group

    def theirs(group):
        return 1 - core + 2 * group

    kv_home = (k_all, dk_all, v_all, dv_all)
    whole = pl.ds(0, BLK)

    def kv_source(tensor, block, cols):
        if tensor < 2:
            return (kn, dkn)[tensor].at[block, :, cols]
        first = pl.multiple_of(block * BLK + cols.start, 128)
        return (v_in if tensor == 2 else dv_in).at[:, pl.ds(first, cols.size)]

    def kv_far(head, tensor, which):
        group, cols = head // 5, pl.ds(head % 5 * HDIM, HDIM)
        return remote(
            kv_source(tensor, theirs(group) if which else mine(group), cols),
            kv_home[tensor].at[group, pl.ds((2 + which) * ROWS, ROWS), cols],
            far_send.at[which],
            far_recv.at[head, which],
            ("lo", "cross")[which],
        )

    def kv_mate(group, tensor):
        return remote(
            kv_source(tensor, theirs(group), whole),
            kv_home[tensor].at[group, pl.ds(ROWS, ROWS), :],
            kv_send.at[group, tensor],
            kv_recv.at[group, tensor],
            "mate",
        )

    def kv_own(group, tensor):
        return pltpu.make_async_copy(
            kv_source(tensor, mine(group), whole),
            kv_home[tensor].at[group, pl.ds(0, ROWS), :],
            own_sem.at[group, tensor],
        )

    q_from, q_home = (qn, dqn), (q_all, dq_all)

    def q_copy(group, tensor):
        return remote(
            q_from[tensor].at[theirs(group)],
            q_home[tensor].at[group, pl.ds(ROWS, ROWS), :],
            q_send.at[group, tensor],
            q_recv.at[group, tensor],
            "mate",
        )

    def q_own(group, tensor):
        return pltpu.make_async_copy(
            q_from[tensor].at[mine(group)],
            q_home[tensor].at[group, pl.ds(0, ROWS), :],
            own_sem.at[group, 4 + tensor],
        )

    def send_far(head):
        for tensor in (2, 3, 0, 1):
            for which in range(2):
                kv_far(head, tensor, which).start()

    def start_keys():
        for head in range(4):
            send_far(head)
        for group in range(2):
            for tensor in range(4):
                kv_mate(group, tensor).start()
                kv_own(group, tensor).start()

    def start_queries():
        for group in range(2):
            for tensor in range(2):
                q_copy(group, tensor).start()
                q_own(group, tensor).start()

    def wait_group(group):
        for tensor in range(4):
            kv_own(group, tensor).wait()
            kv_mate(group, tensor).wait_recv()
        for tensor in range(2):
            q_own(group, tensor).wait()
            q_copy(group, tensor).wait_recv()

    factor = HDIM ** (-0.5)
    nt = (((1,), (1,)), ((), ()))

    def head(number):
        if number + 4 < 10:
            send_far(number + 4)
        group, cols = number // 5, pl.ds(number % 5 * HDIM, HDIM)
        if number % 5 == 0:
            wait_group(group)
        for which in range(2):
            four = k_all.at[group, :, cols]
            pltpu.make_async_copy(four, four, far_recv.at[number, which]).wait()
        queries, dual_queries = q_all[group, :, cols], dq_all[group, :, cols]
        keys, dual_keys = k_all[group, :, cols], dk_all[group, :, cols]
        values, dual_values = v_all[group, :, cols], dv_all[group, :, cols]
        scores = lax.dot_general(queries, keys, nt, preferred_element_type=F32) * factor
        dual_scores = (
            lax.dot_general(
                jnp.concatenate([dual_queries, queries], axis=1),
                jnp.concatenate([keys, dual_keys], axis=1),
                nt,
                preferred_element_type=F32,
            )
            * factor
        )
        raised = jnp.exp(scores - jnp.max(scores, axis=-1, keepdims=True))
        probs = raised * (1.0 / jnp.sum(raised, axis=-1, keepdims=True))
        spread = probs * (dual_scores - jnp.sum(probs * dual_scores, axis=-1, keepdims=True))
        low = probs.astype(BF16)
        both = jnp.dot(
            low, jnp.concatenate([values, dual_values], axis=1), preferred_element_type=F32
        )
        dual = both[:, HDIM:] + jnp.dot(spread.astype(BF16), values, preferred_element_type=F32)
        plain = both[:, :HDIM].astype(BF16)
        dual = dual.astype(BF16)
        for owner in range(2):
            rows = slice(owner * ROWS, (owner + 1) * ROWS)
            attn[group, pl.ds(owner * 256, ROWS), cols] = plain[rows]
            attn[group, pl.ds(owner * 256 + ROWS, ROWS), cols] = dual[rows]

    def plane_of(index):
        return z_at(-Z_OFFS[index])

    def product(group, plane, low=0, high=BLK):
        first = pl.multiple_of(plane * 8, 8)
        cols = pl.ds(low, high - low)
        weight = w_all[group, pl.ds(first, 8), :, cols].reshape(PLANE, high - low)
        return lax.dot_general(attn[group, :, cols], weight, nt, preferred_element_type=F32)

    def out_copies(index):
        first = pl.multiple_of(plane_of(index) * PLANE, 128)
        cols = pl.ds(first, PLANE)
        copies = []
        for half in range(2):
            rows = pl.ds(half * ROWS, ROWS)
            copies.append(
                remote(
                    give.at[index, rows, :],
                    (got, dual_got)[half].at[:, cols],
                    part_send.at[index, half],
                    part_recv.at[plane_of(index), half],
                    "mate",
                )
            )
            copies.append(
                pltpu.make_async_copy(
                    keep.at[index, rows, :], (out, dual_out)[half].at[:, cols], out_sem.at[index, half]
                )
            )
        return copies

    def hand_over(index, total):
        give[index] = total[256:].astype(BF16)
        keep[index] = total[:256].astype(BF16)
        for copy in out_copies(index):
            copy.start()

    def project(kind, index):
        plane = plane_of(index)
        if kind == FIRST:
            acc[index] = product(0, plane)
        elif kind == MIDDLE:
            acc[index] += product(1, plane, 0, 384)
        elif kind == LAST:
            hand_over(index, acc[index] + product(1, plane, 384, BLK))
        elif kind == REST:
            hand_over(index, acc[index] + product(1, plane))
        else:
            hand_over(index, product(0, plane) + product(1, plane))

    for item in ORDER:
        if item >= SEND:
            code, way_out = divmod(item - SEND, 5)
            for copy in w_copies(code, SIDES[way_out]):
                copy.start()
        elif item < SECOND:
            for copy in w_copies(item, "zf"):
                copy.wait_recv()
        elif item == SECOND:
            second()
        elif item == KEY_NORM:
            for which in range(3):
                load(which).wait()
            rms_tangent(k_raw, dk_raw, k_scale, kn, dkn)
        elif item == KEYS:
            start_keys()
        elif item == QUERY_NORM:
            for which in range(3, 6):
                load(which).wait()
            rms_tangent(q_raw, dq_raw, q_scale, qn, dqn)
        elif item == QUERIES:
            start_queries()
        elif item < FIRST:
            head(item - HEAD)
        else:
            project(item // 10 * 10, item % 10)

    lo_w.wait_send()
    for which in range(2):
        pltpu.make_async_copy(k_all, k_all, far_send.at[which]).wait()
    for group in range(2):
        for tensor in range(4):
            kv_mate(group, tensor).wait_send()
        for tensor in range(2):
            q_copy(group, tensor).wait_send()
    for index, (_, (row, rows, col, cols)) in enumerate(PARTS):
        sent = w_all.at[0, pl.ds(0, 63), pl.ds(row, rows), pl.ds(col, cols)]
        pltpu.make_async_copy(sent, sent, w_send.at[index]).wait()
    for index in range(8):
        for copy in out_copies(index):
            copy.wait()


def body(q, k, v, dq, dk, dv, q_gain, k_gain, weight):
    rows, width = q.shape
    hbm = pl.BlockSpec(memory_space=pltpu.HBM)
    free = pl.BlockSpec(memory_space=pl.ANY)
    sem = pltpu.SemaphoreType.DMA
    kv = pltpu.VMEM((2, 4 * ROWS, BLK), BF16)
    qs = pltpu.VMEM((2, 2 * ROWS, BLK), BF16)
    normed = pltpu.VMEM((4, ROWS, BLK), BF16)
    raw = pltpu.VMEM((rows, width), BF16)
    scale = pltpu.VMEM((width,), F32)
    shape = jax.ShapeDtypeStruct((rows, 2 * width), BF16)
    plain, dual, got, dual_got = pl.pallas_call(
        kernel,
        out_shape=(shape,) * 4,
        in_specs=[hbm] * 9,
        out_specs=(free,) * 4,
        scratch_shapes=[
            raw,
            raw,
            raw,
            raw,
            scale,
            scale,
            pltpu.VMEM((2, 64, UNIT, BLK), BF16),
            normed,
            normed,
            normed,
            normed,
            qs,
            qs,
            kv,
            kv,
            kv,
            kv,
            pltpu.VMEM((2, 4 * ROWS, BLK), BF16),
            pltpu.VMEM((8, 4 * ROWS, PLANE), F32),
            pltpu.VMEM((8, 2 * ROWS, PLANE), BF16),
            pltpu.VMEM((8, 2 * ROWS, PLANE), BF16),
            sem((6,)),
            sem((5, 64)),
            sem((5,)),
            sem((3,)),
            sem((10, 2)),
            sem((2,)),
            sem((2, 4)),
            sem((2, 4)),
            sem((2, 2)),
            sem((2, 2)),
            sem((2, 6)),
            sem((8, 2)),
            sem((8, 2)),
            sem((8, 2)),
        ],
        compiler_params=pltpu.CompilerParams(
            collective_id=0, has_side_effects=True, vmem_limit_bytes=44 * 1024 * 1024
        ),
        name="tangent_attention",
    )(*(pltpu.with_memory_space_constraint(a, pltpu.HBM) for a in (q, dq, k, dk, v, dv, q_gain, k_gain, weight.T)))
    return (
        (plain.astype(F32) + got.astype(F32)).astype(BF16),
        (dual.astype(F32) + dual_got.astype(F32)).astype(BF16),
    )


def solution(mesh):
    tokens = P(("dp", "seq"), None)
    return jax.shard_map(
        body,
        mesh=mesh,
        in_specs=(tokens,) * 6 + (P(), P(), P("seq", "dp")),
        out_specs=(tokens, tokens),
        check_vma=False,
    )
```

```python
import jax
import jax.numpy as jnp
from jax import lax
from jax.experimental import pallas as pl
from jax.experimental.pallas import tpu as pltpu
from jax.sharding import PartitionSpec as P

HDIM = 128
NZ, NY = 8, 4
ROWS = 128
BLK = 640
UNIT = 80
PLANE = 640
EPS = 1e-06
MESH = pl.DeviceIdType.MESH
BF16 = jnp.bfloat16
F32 = jnp.float32

Z_OFFS = (0, 1, -1, 2, -2, 3, -3, 4)
Y_OFFS = (0, 1, -1, 2)
SECOND, KEY_NORM, KEYS, QUERY_NORM, QUERIES, HEAD = 400, 401, 402, 403, 404, 500
FIRST, MIDDLE, LAST, REST, WHOLE = 600, 610, 620, 630, 640
SEND = 1000
SIDES = ("hi", "yf", "yb", "zf", "zb")
STREAMS = (
    (True, ((0, 32, 0, 512),)),
    (False, ((0, 32, 0, 640),)),
    (True, ((32, 48, 0, 640), (0, 32, 512, 128))),
    (False, ((32, 48, 0, 640),)),
)
PARTS = tuple((stream, part) for stream, (_, parts) in enumerate(STREAMS) for part in parts)
ORDER = (
    1003, 1004, 1641, 1642, 1640, 1643, 1644, 1001, 1002, 1000, 401, 402, 8, 1043, 16, 1084, 1041,
    1042, 1040, 1081, 1082, 1080, 130, 1653, 132, 1654, 1663, 1664, 1651, 129, 136, 400, 144, 2, 4,
    1647, 1960, 1646, 1322, 1320, 1323, 1324, 1321, 1962, 1010, 403, 1963, 1964, 1961, 1020, 404,
    24, 1122, 32, 10, 1123, 12, 1164, 1120, 1162, 1121, 18, 20, 1648, 1160, 1649, 1161, 138, 146,
    1050, 134, 1673, 1060, 1674, 133, 1011, 193, 1967, 1968, 140, 1090, 1969, 148, 68, 1051, 131,
    1100, 72, 1362, 500, 80, 66, 1402, 1363, 1404, 1656, 1340, 1361, 1360, 200, 2002, 208, 28, 2042,
    1401, 194, 1400, 40, 2003, 48, 36, 2044, 1202, 26, 1330, 1201, 34, 1668, 137, 1669, 1242, 145,
    1140, 6, 1241, 1658, 76, 1659, 1200, 14, 1091, 142, 150, 84, 1240, 1203, 501, 135, 201, 2007,
    1966, 1679, 209, 2047, 1331, 1180, 1130, 74, 2008, 2001, 88, 2049, 1442, 96, 1170, 1482, 82,
    1030, 1441, 216, 1443, 44, 42, 224, 1484, 2082, 1380, 1481, 1678, 52, 50, 1070, 2122, 22, 141,
    149, 2124, 1420, 2041, 2083, 502, 195, 139, 147, 1370, 1683, 1724, 1131, 1440, 70, 56, 1282,
    1281, 1734, 92, 1480, 1693, 151, 202, 217, 2087, 1171, 100, 1744, 1410, 2088, 2006, 90, 104,
    225, 1522, 2127, 1220, 1521, 2129, 98, 112, 1562, 1210, 1561, 1523, 143, 1260, 210, 240, 2202,
    1729, 503, 60, 232, 30, 1703, 2046, 2162, 1250, 1110, 1371, 58, 160, 1754, 1350, 1688, 38, 152,
    1411, 1280, 108, 1713, 1749, 162, 1460, 203, 2081, 154, 1500, 106, 1708, 1739, 1211, 164, 116,
    1450, 233, 2167, 2121, 114, 1520, 120, 241, 1602, 1698, 1759, 2207, 504, 211, 1601, 1490, 1251,
    156, 1718, 161, 78, 1804, 1560, 86, 2086, 1300, 153, 2163, 166, 1814, 1451, 218, 2126, 1150, 46,
    1491, 124, 1290, 158, 2168, 165, 1824, 2201, 1190, 2161, 226, 505, 157, 122, 163, 54, 1291,
    1540, 1763, 1809, 1531, 1530, 219, 2166, 1580, 1773, 155, 94, 167, 1834, 1571, 2206, 1570, 227,
    1783, 102, 1611, 1600, 159, 1829, 1971, 242, 1390, 1976, 234, 1768, 248, 2242, 2241, 62, 1819,
    1430, 110, 506, 249, 235, 118, 2247, 1793, 1839, 2246, 1230, 1620, 2011, 243, 168, 1788, 126,
    1610, 2051, 1270, 2016, 170, 1778, 1470, 2056, 2091, 1510, 172, 1798, 2131, 1310, 250, 507, 251,
    169, 1843, 2096, 1550, 2136, 1853, 1590, 2211, 1863, 1, 65, 3, 196, 5, 197, 69, 67, 7, 71, 198,
    199, 174, 2171, 1630, 600, 1848, 610, 173, 1873, 2176, 2216, 171, 1868, 2251, 175, 1858, 2256,
    508, 1878, 9, 11, 13, 204, 73, 205, 77, 15, 75, 79, 206, 207, 601, 611, 17, 19, 21, 212, 81,
    213, 85, 83, 23, 87, 214, 215, 602, 612, 25, 29, 27, 220, 89, 221, 93, 91, 31, 222, 95, 223,
    603, 613, 33, 37, 35, 228, 97, 229, 101, 99, 39, 230, 103, 231, 604, 614, 509, 620, 621, 622,
    623, 624, 41, 45, 43, 236, 237, 105, 109, 107, 47, 111, 238, 239, 645, 49, 53, 51, 244, 245,
    113, 176, 178, 180, 117, 177, 115, 182, 181, 179, 183, 55, 246, 119, 247, 646, 57, 61, 59, 252,
    121, 253, 125, 123, 63, 184, 186, 188, 185, 127, 190, 254, 189, 255, 187, 191, 647,
)


def rms_tangent(primal_ref, tangent_ref, gain_ref, normed_ref, dual_ref):
    width = primal_ref.shape[1]
    for row in range(0, ROWS, 32):
        rows = pl.ds(row, 32)
        primal = primal_ref[rows, :].astype(F32)
        tangent = tangent_ref[rows, :].astype(F32)
        inverse = lax.rsqrt(jnp.sum(primal * primal, axis=-1, keepdims=True) * (1.0 / width) + EPS)
        across = jnp.sum(primal * tangent, axis=-1, keepdims=True) * (1.0 / width)
        pull = inverse * inverse * inverse * across
        gain = gain_ref[...].reshape(1, width)
        normed = (primal * inverse * gain).astype(BF16)
        dual = (gain * (tangent * inverse - primal * pull)).astype(BF16)
        for block in range(4):
            normed_ref[block, rows, :] = normed[:, block * BLK : (block + 1) * BLK]
            dual_ref[block, rows, :] = dual[:, block * BLK : (block + 1) * BLK]


def kernel(
    q_in,
    dq_in,
    k_in,
    dk_in,
    v_in,
    dv_in,
    q_gain,
    k_gain,
    w_in,
    out,
    dual_out,
    got,
    dual_got,
    q_raw,
    dq_raw,
    k_raw,
    dk_raw,
    q_scale,
    k_scale,
    w_all,
    qn,
    dqn,
    kn,
    dkn,
    q_all,
    dq_all,
    k_all,
    dk_all,
    v_all,
    dv_all,
    attn,
    acc,
    give,
    keep,
    load_sem,
    w_recv,
    w_send,
    first_sem,
    far_recv,
    far_send,
    kv_recv,
    kv_send,
    q_recv,
    q_send,
    own_sem,
    part_recv,
    part_send,
    out_sem,
):
    def load(which):
        source, home = loads[which]
        return pltpu.make_async_copy(source, home, load_sem.at[which])

    loads = (
        (k_in, k_raw),
        (dk_in, dk_raw),
        (k_gain, k_scale),
        (q_in, q_raw),
        (dq_in, dq_raw),
        (q_gain, q_scale),
    )
    for which in range(6):
        load(which).start()

    dp = lax.axis_index("dp")
    seq = lax.axis_index("seq")
    z, y, hi = dp // 8, lax.rem(dp // 2, 4), lax.rem(dp, 2)
    lo, core = seq // 2, lax.rem(seq, 2)
    way = 1 - 2 * core

    def unit(zz, yy, hh):
        return zz * 8 + yy * 2 + hh

    def z_at(off):
        return lax.rem(z + off * way + NZ, NZ)

    def y_at(off):
        return lax.rem(y + off * way + NY, NY)

    side = {
        "zf": (unit(z_at(1), y, hi), seq),
        "zb": (unit(z_at(-1), y, hi), seq),
        "yf": (unit(z, y_at(1), hi), seq),
        "yb": (unit(z, y_at(-1), hi), seq),
        "hi": (unit(z, y, 1 - hi), (1 - lo) * 2 + core),
        "lo": (dp, (1 - lo) * 2 + core),
        "cross": (dp, (1 - lo) * 2 + 1 - core),
        "mate": (dp, lo * 2 + 1 - core),
    }

    barrier = pltpu.get_barrier_semaphore()
    for target in side.values():
        pl.semaphore_signal(barrier, inc=1, device_id=target, device_id_type=MESH)
    pl.semaphore_wait(barrier, len(side))

    def remote(src, dst, send_sem, recv_sem, to):
        return pltpu.make_async_remote_copy(
            src_ref=src,
            dst_ref=dst,
            send_sem=send_sem,
            recv_sem=recv_sem,
            device_id=side[to],
            device_id_type=MESH,
        )

    own_w = pltpu.make_async_copy(w_in, w_all.at[lo, dp], first_sem.at[0])
    lo_w = remote(w_in, w_all.at[lo, dp], first_sem.at[1], first_sem.at[2], "lo")

    def src(zo, yo, flip):
        return unit(z_at(-zo), y_at(-yo), 1 - hi if flip else hi)

    def w_copies(code, to):
        stream, rest = divmod(code, 64)
        zo, rest = divmod(rest, 8)
        yo, flip = divmod(rest, 2)
        source = src(Z_OFFS[zo], Y_OFFS[yo], flip)
        began = STREAMS[stream][0]
        block = lo if began != (flip == 1) else 1 - lo
        copies = []
        for index, (owner, (row, rows, col, cols)) in enumerate(PARTS):
            if owner != stream:
                continue
            where = w_all.at[block, source, pl.ds(row, rows), pl.ds(col, cols)]
            held = where
            if began and rest == 0 and zo == 0:
                held = w_in.at[pl.ds(row, rows), pl.ds(col, cols)]
            copies.append(remote(held, where, w_send.at[index], w_recv.at[index, source], to))
        return copies

    lo_w.start()
    own_w.start()

    def second():
        own_w.wait()
        lo_w.wait_recv()

    def mine(group):
        return core + 2 * group

    def theirs(group):
        return 1 - core + 2 * group

    kv_home = (k_all, dk_all, v_all, dv_all)
    whole = pl.ds(0, BLK)

    def kv_source(tensor, block, cols):
        if tensor < 2:
            return (kn, dkn)[tensor].at[block, :, cols]
        first = pl.multiple_of(block * BLK + cols.start, 128)
        return (v_in if tensor == 2 else dv_in).at[:, pl.ds(first, cols.size)]

    def kv_far(head, tensor, which):
        group, cols = head // 5, pl.ds(head % 5 * HDIM, HDIM)
        return remote(
            kv_source(tensor, theirs(group) if which else mine(group), cols),
            kv_home[tensor].at[group, pl.ds((2 + which) * ROWS, ROWS), cols],
            far_send.at[which],
            far_recv.at[head, which],
            ("lo", "cross")[which],
        )

    def kv_mate(group, tensor):
        return remote(
            kv_source(tensor, theirs(group), whole),
            kv_home[tensor].at[group, pl.ds(ROWS, ROWS), :],
            kv_send.at[group, tensor],
            kv_recv.at[group, tensor],
            "mate",
        )

    def kv_own(group, tensor):
        return pltpu.make_async_copy(
            kv_source(tensor, mine(group), whole),
            kv_home[tensor].at[group, pl.ds(0, ROWS), :],
            own_sem.at[group, tensor],
        )

    q_from, q_home = (qn, dqn), (q_all, dq_all)

    def q_copy(group, tensor):
        return remote(
            q_from[tensor].at[theirs(group)],
            q_home[tensor].at[group, pl.ds(ROWS, ROWS), :],
            q_send.at[group, tensor],
            q_recv.at[group, tensor],
            "mate",
        )

    def q_own(group, tensor):
        return pltpu.make_async_copy(
            q_from[tensor].at[mine(group)],
            q_home[tensor].at[group, pl.ds(0, ROWS), :],
            own_sem.at[group, 4 + tensor],
        )

    def send_far(head):
        for tensor in (2, 3, 0, 1):
            for which in range(2):
                kv_far(head, tensor, which).start()

    def start_keys():
        for head in range(4):
            send_far(head)
        for group in range(2):
            for tensor in range(4):
                kv_mate(group, tensor).start()
                kv_own(group, tensor).start()

    def start_queries():
        for group in range(2):
            for tensor in range(2):
                q_copy(group, tensor).start()
                q_own(group, tensor).start()

    def wait_group(group):
        for tensor in range(4):
            kv_own(group, tensor).wait()
            kv_mate(group, tensor).wait_recv()
        for tensor in range(2):
            q_own(group, tensor).wait()
            q_copy(group, tensor).wait_recv()

    factor = HDIM ** (-0.5)
    nt = (((1,), (1,)), ((), ()))

    def head(number):
        if number + 4 < 10:
            send_far(number + 4)
        group, cols = number // 5, pl.ds(number % 5 * HDIM, HDIM)
        if number % 5 == 0:
            wait_group(group)
        for which in range(2):
            four = k_all.at[group, :, cols]
            pltpu.make_async_copy(four, four, far_recv.at[number, which]).wait()
        queries, dual_queries = q_all[group, :, cols], dq_all[group, :, cols]
        keys, dual_keys = k_all[group, :, cols], dk_all[group, :, cols]
        values, dual_values = v_all[group, :, cols], dv_all[group, :, cols]
        scores = lax.dot_general(queries, keys, nt, preferred_element_type=F32) * factor
        dual_scores = (
            lax.dot_general(
                jnp.concatenate([dual_queries, queries], axis=1),
                jnp.concatenate([keys, dual_keys], axis=1),
                nt,
                preferred_element_type=F32,
            )
            * factor
        )
        raised = jnp.exp(scores - jnp.max(scores, axis=-1, keepdims=True))
        probs = raised * (1.0 / jnp.sum(raised, axis=-1, keepdims=True))
        spread = probs * (dual_scores - jnp.sum(probs * dual_scores, axis=-1, keepdims=True))
        low = probs.astype(BF16)
        both = jnp.dot(
            low, jnp.concatenate([values, dual_values], axis=1), preferred_element_type=F32
        )
        dual = both[:, HDIM:] + jnp.dot(spread.astype(BF16), values, preferred_element_type=F32)
        plain = both[:, :HDIM].astype(BF16)
        dual = dual.astype(BF16)
        for owner in range(2):
            rows = slice(owner * ROWS, (owner + 1) * ROWS)
            attn[group, pl.ds(owner * 256, ROWS), cols] = plain[rows]
            attn[group, pl.ds(owner * 256 + ROWS, ROWS), cols] = dual[rows]

    def plane_of(index):
        return z_at(-Z_OFFS[index])

    def product(group, plane, low=0, high=BLK):
        first = pl.multiple_of(plane * 8, 8)
        cols = pl.ds(low, high - low)
        weight = w_all[group, pl.ds(first, 8), :, cols].reshape(PLANE, high - low)
        return lax.dot_general(attn[group, :, cols], weight, nt, preferred_element_type=F32)

    def out_copies(index):
        first = pl.multiple_of(plane_of(index) * PLANE, 128)
        cols = pl.ds(first, PLANE)
        copies = []
        for half in range(2):
            rows = pl.ds(half * ROWS, ROWS)
            copies.append(
                remote(
                    give.at[index, rows, :],
                    (got, dual_got)[half].at[:, cols],
                    part_send.at[index, half],
                    part_recv.at[plane_of(index), half],
                    "mate",
                )
            )
            copies.append(
                pltpu.make_async_copy(
                    keep.at[index, rows, :], (out, dual_out)[half].at[:, cols], out_sem.at[index, half]
                )
            )
        return copies

    def hand_over(index, total):
        give[index] = total[256:].astype(BF16)
        keep[index] = total[:256].astype(BF16)
        for copy in out_copies(index):
            copy.start()

    def project(kind, index):
        plane = plane_of(index)
        if kind == FIRST:
            acc[index] = product(0, plane)
        elif kind == MIDDLE:
            acc[index] += product(1, plane, 0, 384)
        elif kind == LAST:
            hand_over(index, acc[index] + product(1, plane, 384, BLK))
        elif kind == REST:
            hand_over(index, acc[index] + product(1, plane))
        else:
            hand_over(index, product(0, plane) + product(1, plane))

    for item in ORDER:
        if item >= SEND:
            code, way_out = divmod(item - SEND, 5)
            for copy in w_copies(code, SIDES[way_out]):
                copy.start()
        elif item < SECOND:
            for copy in w_copies(item, "zf"):
                copy.wait_recv()
        elif item == SECOND:
            second()
        elif item == KEY_NORM:
            for which in range(3):
                load(which).wait()
            rms_tangent(k_raw, dk_raw, k_scale, kn, dkn)
        elif item == KEYS:
            start_keys()
        elif item == QUERY_NORM:
            for which in range(3, 6):
                load(which).wait()
            rms_tangent(q_raw, dq_raw, q_scale, qn, dqn)
        elif item == QUERIES:
            start_queries()
        elif item < FIRST:
            head(item - HEAD)
        else:
            project(item // 10 * 10, item % 10)

    lo_w.wait_send()
    for which in range(2):
        pltpu.make_async_copy(k_all, k_all, far_send.at[which]).wait()
    for group in range(2):
        for tensor in range(4):
            kv_mate(group, tensor).wait_send()
        for tensor in range(2):
            q_copy(group, tensor).wait_send()
    for index, (_, (row, rows, col, cols)) in enumerate(PARTS):
        sent = w_all.at[0, pl.ds(0, 63), pl.ds(row, rows), pl.ds(col, cols)]
        pltpu.make_async_copy(sent, sent, w_send.at[index]).wait()
    for index in range(8):
        for copy in out_copies(index):
            copy.wait()


def add_sums(plain, dual, got, dual_got, out, dual_out, total, sems):
    def copy(half, part):
        rows = pl.ds(part * 16, 16)
        return pltpu.make_async_copy(
            total.at[half, rows, :], (out, dual_out)[half].at[rows, :], sems.at[half, part]
        )

    for part in range(8):
        rows = pl.ds(part * 16, 16)
        for half, (mine, theirs) in enumerate(((plain, got), (dual, dual_got))):
            total[half, rows, :] = (mine[rows, :].astype(F32) + theirs[rows, :].astype(F32)).astype(BF16)
            copy(half, part).start()
    for part in range(8):
        for half in range(2):
            copy(half, part).wait()


def body(q, k, v, dq, dk, dv, q_gain, k_gain, weight):
    rows, width = q.shape
    hbm = pl.BlockSpec(memory_space=pltpu.HBM)
    free = pl.BlockSpec(memory_space=pl.ANY)
    sem = pltpu.SemaphoreType.DMA
    kv = pltpu.VMEM((2, 4 * ROWS, BLK), BF16)
    qs = pltpu.VMEM((2, 2 * ROWS, BLK), BF16)
    normed = pltpu.VMEM((4, ROWS, BLK), BF16)
    raw = pltpu.VMEM((rows, width), BF16)
    scale = pltpu.VMEM((width,), F32)
    shape = jax.ShapeDtypeStruct((rows, 2 * width), BF16)
    plain, dual, got, dual_got = pl.pallas_call(
        kernel,
        out_shape=(shape,) * 4,
        in_specs=[hbm] * 9,
        out_specs=(free,) * 4,
        scratch_shapes=[
            raw,
            raw,
            raw,
            raw,
            scale,
            scale,
            pltpu.VMEM((2, 64, UNIT, BLK), BF16),
            normed,
            normed,
            normed,
            normed,
            qs,
            qs,
            kv,
            kv,
            kv,
            kv,
            pltpu.VMEM((2, 4 * ROWS, BLK), BF16),
            pltpu.VMEM((8, 4 * ROWS, PLANE), F32),
            pltpu.VMEM((8, 2 * ROWS, PLANE), BF16),
            pltpu.VMEM((8, 2 * ROWS, PLANE), BF16),
            sem((6,)),
            sem((5, 64)),
            sem((5,)),
            sem((3,)),
            sem((10, 2)),
            sem((2,)),
            sem((2, 4)),
            sem((2, 4)),
            sem((2, 2)),
            sem((2, 2)),
            sem((2, 6)),
            sem((8, 2)),
            sem((8, 2)),
            sem((8, 2)),
        ],
        compiler_params=pltpu.CompilerParams(
            collective_id=0, has_side_effects=True, vmem_limit_bytes=44 * 1024 * 1024
        ),
        name="tangent_attention",
    )(*(pltpu.with_memory_space_constraint(a, pltpu.HBM) for a in (q, dq, k, dk, v, dv, q_gain, k_gain, weight.T)))
    vmem = pl.BlockSpec(memory_space=pltpu.VMEM)
    return pl.pallas_call(
        add_sums,
        out_shape=(shape, shape),
        in_specs=[vmem] * 4,
        out_specs=(hbm, hbm),
        scratch_shapes=[pltpu.VMEM((2, rows, 2 * width), BF16), sem((2, 8))],
        compiler_params=pltpu.CompilerParams(vmem_limit_bytes=16 * 1024 * 1024),
        name="add_sums",
    )(plain, dual, got, dual_got)


def solution(mesh):
    tokens = P(("dp", "seq"), None)
    return jax.shard_map(
        body,
        mesh=mesh,
        in_specs=(tokens,) * 6 + (P(), P(), P("seq", "dp")),
        out_specs=(tokens, tokens),
        check_vma=False,
    )
```
